256 devices in a mesh: dp: 8 (over y_lo, x), space: 32 (over z, y_hi, core).
Axes of the slice: x: 4, y: 4 (y_hi: 2, y_lo: 2; y = y_hi * 2 + y_lo), z: 8, core: 2. Of those that a mesh axis runs over, the one named last changes fastest.
Arguments:
- volumes: bfloat16 [8, 32, 64, 48, 128], P('dp', None, 'space'), may hold values from -6 to 6
- kernel: bfloat16 [3, 3, 3, 64, 32], replicated, may hold values from -0.21875 to 0.21875
- bias: float32 [64], replicated, may hold values from -3 to 3
- cotangent: bfloat16 [8, 64, 64, 48, 128], P('dp', None, 'space'), may hold values from -6 to 6
- finished_grads: float32 [8, 32, 262144], P('dp', 'space'), may hold values from -0.5 to 0.5
Outputs:
- activations: bfloat16 [8, 64, 64, 48, 128], P('dp', None, 'space')
- grad_volumes: bfloat16 [8, 32, 64, 48, 128], P('dp', None, 'space')
- grad_kernel: float32 [3, 3, 3, 64, 32], replicated
- grad_bias: float32 [64], replicated
- summed_grads: float32 [262144], replicated
The draws below stay inside these ranges and needn't reach their ends.
All inputs are finite; a program needn't handle non-finite values.
Results may differ from the reference program's by a relative error of at most 0.006.
Values may be sent and summed in bfloat16 or wider, within the bound.
No kernel may reach another device: no remote copies, remote signals or barrier semaphores. Data moves between devices by JAX's collectives and lax.ppermute only.
A program may use at most 128 MiB of HBM per device.

```python
import math
import jax
import jax.numpy as jnp
from jax import lax

C_IN = 32
C_OUT = 64
CY = 48
CX = 128
GRADS = 262144
BATCH = 8
NZ = 64
N_DP = 8
N_SPACE = 32


def block_scale(key, extent, shards, low, largest):
    def one(axis_at, blocks):
        steps = jax.random.uniform(jax.random.fold_in(jax.random.fold_in(key, 6), axis_at), (blocks,), jnp.float32, low / len(shards), largest / len(shards))
        return jnp.repeat(jnp.exp(steps), extent[axis_at] // blocks).reshape((-1,) + (1,) * (len(extent) - axis_at - 1))

    gain = one(*shards[0])
    for cut in shards[1:]:
        gain = gain * one(*cut)
    return gain


def gaussian(rng, extent, scale, limit, shards=(), held_as=jnp.bfloat16):
    array = scale * jax.random.normal(rng, extent, jnp.float32)
    if shards:
        array = array * block_scale(rng, extent, shards, -0.22, 0.18)
    return jnp.clip(array, -limit, limit).astype(held_as)


def setup_inputs(seed: int = 0) -> dict:
    key_list = jax.random.split(jax.random.key(seed), 6)
    volumes = gaussian(key_list[0], (BATCH, C_IN, NZ, CY, CX), 1.0, 6.0, ((0, 8), (2, 32)))
    kernel = gaussian(key_list[1], (3, 3, 3, C_OUT, C_IN), (27 * C_IN) ** -0.5, 0.21875)
    bias = gaussian(key_list[2], (C_OUT,), 0.5, 3.0, (), jnp.float32)
    cotangent = gaussian(key_list[3], (BATCH, C_OUT, NZ, CY, CX), 1.0, 6.0, ((0, 8), (2, 32)))
    finished_grads = gaussian(key_list[4], (N_DP, N_SPACE, GRADS), 0.0625, 0.5, ((0, 8), (1, 32)), jnp.float32)
    return {"volumes": volumes, "kernel": kernel, "bias": bias, "cotangent": cotangent, "finished_grads": finished_grads}


def convolve(field, weights):
    return lax.conv_general_dilated(field[None], weights, (1, 1, 1), [(1, 1), (1, 1), (1, 1)], dimension_numbers=('NCDHW', 'OIDHW', 'NCDHW'), preferred_element_type=jnp.float32)[0]

def reference(volumes, kernel, bias, cotangent, finished_grads):
    forward_w = kernel.transpose(3, 4, 0, 1, 2)
    backward_w = kernel[::-1, ::-1, ::-1].transpose(4, 3, 0, 1, 2)

    def one_sample(pair):
        volume, cot_one = pair
        preact = convolve(volume, forward_w) + bias[:, None, None, None]
        activation = (0.3 * preact + 0.7 * jax.nn.softplus(preact)).astype(jnp.bfloat16)
        grad_pre = (cot_one.astype(jnp.float32) * (0.3 + 0.7 * jax.nn.sigmoid(preact))).astype(jnp.bfloat16)
        grad_input = convolve(grad_pre, backward_w).astype(jnp.bfloat16)
        padded = jnp.pad(volume, ((0, 0), (1, 1), (1, 1), (1, 1)))
        grad_flat = grad_pre.reshape(C_OUT, -1)
        taps = []
        for depth_tap in range(3):
            for row_tap in range(3):
                for col_tap in range(3):
                    shifted = padded[:, depth_tap:depth_tap + NZ, row_tap:row_tap + CY, col_tap:col_tap + CX].reshape(C_IN, -1)
                    taps.append(jnp.dot(grad_flat, shifted.T, preferred_element_type=jnp.float32))
        grad_taps = jnp.stack(taps).reshape(3, 3, 3, C_OUT, C_IN)
        bias_terms = lax.optimization_barrier(jnp.sum(grad_pre.astype(jnp.float32), axis=(1, 2, 3)))
        return (activation, grad_input, grad_taps, bias_terms)
    activations, grad_volumes, grad_taps, bias_terms = lax.map(one_sample, (volumes, cotangent))
    scale = 1.0 / math.sqrt(BATCH * NZ * CY * CX)
    grad_kernel = lax.optimization_barrier(jnp.sum(grad_taps, axis=0)) * scale
    grad_bias = lax.optimization_barrier(jnp.sum(bias_terms, axis=0)) * scale
    summed_grads = lax.optimization_barrier(jnp.sum(finished_grads, axis=(0, 1)))
    return (activations, grad_volumes, grad_kernel, grad_bias, summed_grads)
```

```python
import math

import jax
import jax.numpy as jnp
from jax import lax
from jax.experimental import pallas as pl
from jax.experimental.pallas import tpu as pltpu
from jax.sharding import Mesh, PartitionSpec as P

BF = jnp.bfloat16
F32 = jnp.float32
CI, CO, NY, NX = 32, 64, 48, 128
PADY = NY + 2
PLANE = ("yl", "x", "yh", "c")
COLUMN = "z"
CHUNKS, COLS = 32, 8
FROWS, TROWS = 64, 16
SPACE = ("z", "yh", "c")


def call(body, outs, scratch, specs, flops, nbytes, out_specs=None):
    return pl.pallas_call(
        body,
        out_shape=outs,
        in_specs=specs,
        out_specs=out_specs or jax.tree.map(lambda _: VM, outs),
        scratch_shapes=scratch,
        compiler_params=pltpu.CompilerParams(vmem_limit_bytes=48 << 20),
        cost_estimate=pl.CostEstimate(flops=flops, transcendentals=0, bytes_accessed=nbytes),
    )


VM = pl.BlockSpec(memory_space=pltpu.VMEM)
HBM = pl.BlockSpec(memory_space=pltpu.HBM)
ANY = pl.BlockSpec(memory_space=pl.ANY)
DMA = pltpu.SemaphoreType.DMA


def turn_kernel(x_ref, p0_ref, p1_ref, x, s0, s1, b0, b1, in_sem, out_sem):
    parts = [
        pltpu.make_async_copy(x_ref.at[pl.ds(8 * n, 8)], x.at[pl.ds(8 * n, 8)], in_sem.at[n])
        for n in range(4)
    ]
    for part in parts:
        part.start()
    for b in (b0, b1):
        b[0:CI, :] = jnp.zeros((CI, NX), BF)
        b[CI * (NY + 1) : CI * PADY, :] = jnp.zeros((CI, NX), BF)
    for n, part in enumerate(parts):
        part.wait()
        for c in range(8 * n, 8 * n + 8):
            for z, s in ((0, s0), (1, s1)):
                s[pl.ds(c, NY, stride=CI), :] = x[c, z].astype(F32)
    outs = []
    for n, (p, s, b) in enumerate(((p0_ref, s0, b0), (p1_ref, s1, b1))):
        b[CI : CI * (NY + 1), :] = s[...].astype(BF)
        outs.append(pltpu.make_async_copy(b, p, out_sem.at[n]))
        outs[-1].start()
    for out in outs:
        out.wait()


def shifted_sum(before, middle, after):
    lane = lax.broadcasted_iota(jnp.int32, middle.shape, 1)
    left = jnp.where(lane == 0, 0.0, pltpu.roll(before, 1, 1))
    right = jnp.where(lane == NX - 1, 0.0, pltpu.roll(after, NX - 1, 1))
    return middle + left + right


HALF = NY // 2 + 2


def halves(planes, buffers, width, sems):
    first, second = [], []
    for n, (p, b) in enumerate(zip(planes, buffers)):
        for part, rows, at in ((first, pl.ds(0, HALF * width), 0), (second, pl.ds(HALF * width, (PADY - HALF) * width), 1)):
            part.append(pltpu.make_async_copy(p.at[rows], b.at[rows], sems.at[2 * n + at]))
    for copy in first + second:
        copy.start()
    return first, second


def forward_kernel(*refs):
    p_refs, (a_ref, bias_ref, cot_ref, act_ref, g0_ref, g1_ref) = refs[:4], refs[4:10]
    planes, (a, cot, act, g0, g1, s0, s1, in_sem, act_sem) = refs[10:14], refs[14:]
    a_copy = pltpu.make_async_copy(a_ref, a, in_sem.at[8])
    a_copy.start()
    first, second = halves(p_refs, planes, CI, in_sem)
    cot_copy = pltpu.make_async_copy(cot_ref, cot, in_sem.at[9])
    cot_copy.start()
    for g in (g0, g1):
        g[0:CO, :] = jnp.zeros((CO, NX), BF)
        g[CO * (NY + 1) : CO * PADY, :] = jnp.zeros((CO, NX), BF)

    def conv(q, _):
        sides = []
        for h in range(2):
            start = pl.multiple_of((2 * q + h) * (2 * CI), 2 * CI)
            sides.append(jnp.concatenate([p[pl.ds(start, 4 * CI), :] for p in planes], axis=0))
        rhs = jnp.concatenate(sides, axis=1)
        r = jnp.dot(a[...], rhs, preferred_element_type=F32)
        for h in range(2):
            rr = r[:, NX * h : NX * (h + 1)]
            y = shifted_sum(rr[0:256], rr[256:512], rr[512:768])
            at = pl.multiple_of((2 * q + h) * 128, 128)
            s0[pl.ds(at, 128), :] = y[0:128]
            s1[pl.ds(at, 128), :] = y[128:256]
        return 0

    a_copy.wait()
    for part, lo in ((first, 0), (second, 6)):
        for copy in part:
            copy.wait()
        lax.fori_loop(lo, lo + 6, conv, 0)
    cot_copy.wait()

    def point(o, _):
        b = bias_ref[o]
        for z, s in ((0, s0), (1, s1)):
            v = s[pl.ds(o, NY, stride=CO), :] + b
            sig = 0.5 + 0.5 * jnp.tanh(0.5 * jnp.abs(v))
            soft = jnp.maximum(v, 0.0) - jnp.log(sig)
            act[o, z] = (0.3 * v + 0.7 * soft).astype(BF)
            slope = 0.3 + 0.7 * jnp.where(v >= 0, sig, 1.0 - sig)
            s[pl.ds(o, NY, stride=CO), :] = cot[o, z].astype(F32) * slope
        return 0

    outs = []
    for n in range(4):
        lax.fori_loop(16 * n, 16 * n + 16, point, 0, unroll=2)
        some = pl.ds(16 * n, 16)
        outs.append(pltpu.make_async_copy(act.at[some], act_ref.at[some], act_sem.at[n]))
        outs[-1].start()
    for n, (g_ref, g, s) in enumerate(((g0_ref, g0, s0), (g1_ref, g1, s1))):
        g[CO : CO * (NY + 1), :] = s[...].astype(BF)
        outs.append(pltpu.make_async_copy(g, g_ref, act_sem.at[4 + n]))
        outs[-1].start()
    for out in outs:
        out.wait()


def weight_kernel(*refs):
    p_refs, g_refs, out_ref = refs[:4], refs[4:6], refs[6]
    planes, gs_buf, acc, sems = refs[7:11], refs[11:13], refs[13], refs[14]
    first, second = halves(p_refs, planes, CI, sems)
    g_first, g_second = halves(g_refs, gs_buf, CO, sems.at[pl.ds(8, 4)])
    acc[...] = jnp.zeros_like(acc)
    lane = lax.broadcasted_iota(jnp.int32, (CO, NX), 1)

    def row(y, _):
        gs, xs = [], []
        ystart = pl.multiple_of(y * CI, CI)
        gstart = pl.multiple_of((y + 1) * CO, CO)
        for z, g in enumerate(gs_buf):
            mid = g[pl.ds(gstart, CO), :]
            wide = mid.astype(F32)
            before = jnp.where(lane == NX - 1, 0.0, pltpu.roll(wide, NX - 1, 1)).astype(BF)
            after = jnp.where(lane == 0, 0.0, pltpu.roll(wide, 1, 1)).astype(BF)
            gs.append(jnp.concatenate([before, mid, after], axis=0))
            xs.append(
                jnp.concatenate(
                    [planes[z + i][pl.ds(ystart, 3 * CI), :] for i in range(3)]
                    + [jnp.ones((16, NX), BF)],
                    axis=0,
                )
            )
        acc[...] += lax.dot_general(
            jnp.concatenate(xs, axis=1),
            jnp.concatenate(gs, axis=1),
            (((1,), (1,)), ((), ())),
            preferred_element_type=F32,
        )
        return 0

    for part, lo in ((first + g_first, 0), (second + g_second, 24)):
        for copy in part:
            copy.wait()
        lax.fori_loop(lo, lo + 24, row, 0, unroll=2)
    out_ref[0:288, :] = acc[0:288, 0:128].astype(BF)
    side = acc[0:288, 128:192]
    tail = jnp.concatenate([side[160:288], jnp.zeros((32, CO), F32)], axis=0)
    out_ref[288:448, :] = jnp.concatenate([side[0:160], tail], axis=1).astype(BF)
    out_ref[448:464, :] = acc[288:304, 0:128].astype(BF)
    out_ref[464:512, :] = jnp.zeros((48, NX), BF)


def back_kernel(*refs):
    p_refs, d_ref, out_ref = refs[:4], refs[4], refs[5]
    planes, (d, buf, s0, s1, sems, out_sem) = refs[6:10], refs[10:]
    d_copy = pltpu.make_async_copy(d_ref, d, sems.at[8])
    d_copy.start()
    first, second = halves(p_refs, planes, CO, sems)

    def conv(q, _):
        for z, s in ((0, s0), (1, s1)):
            sides = []
            for h in range(2):
                start = pl.multiple_of((2 * q + h) * (2 * CO), 2 * CO)
                sides.append(
                    jnp.concatenate(
                        [planes[z + 2 - i][pl.ds(start, 4 * CO), :] for i in range(3)], axis=0
                    )
                )
            r = jnp.dot(d[...], jnp.concatenate(sides, axis=1), preferred_element_type=F32)
            for h in range(2):
                rr = r[:, NX * h : NX * (h + 1)]
                at = pl.multiple_of((2 * q + h) * (2 * CI), 2 * CI)
                s[pl.ds(at, 2 * CI), :] = shifted_sum(rr[128:192], rr[64:128], rr[0:64])
        return 0

    d_copy.wait()
    for part, lo in ((first, 0), (second, 6)):
        for copy in part:
            copy.wait()
        lax.fori_loop(lo, lo + 6, conv, 0)

    def gather(c, _):
        for z, s in ((0, s0), (1, s1)):
            buf[c, z] = s[pl.ds(c, NY, stride=CI), :].astype(BF)
        return 0

    outs = []
    for n in range(2):
        lax.fori_loop(16 * n, 16 * n + 16, gather, 0, unroll=4)
        some = pl.ds(16 * n, 16)
        outs.append(pltpu.make_async_copy(buf.at[some], out_ref.at[some], out_sem.at[n]))
        outs[-1].start()
    for out in outs:
        out.wait()


def prep_kernel(w_ref, f_ref, a_out, d_out, out_ref, turned, a_ref, d_ref, sem):
    out_ref[...] = f_ref[...].reshape(CHUNKS, FROWS, NX).astype(BF)
    for z, hole in ((0, 3), (1, 0)):
        for k in range(3):
            col = (k * 2 + z) * 128
            turned[hole * 128 : hole * 128 + 128, col : col + 128] = jnp.zeros((128, 128), F32)
    for i in range(3):
        for k in range(3):
            w = [w_ref[i, j, k].astype(F32) for j in range(3)]
            none = jnp.zeros((CI, CO), F32)
            for s in range(4):
                pair = jnp.concatenate([w[s] if s < 3 else none, w[s - 1] if s else none], axis=1)
                y, p = ((0, 1), (1, 1), (0, 0), (1, 0))[s]
                row, col = (k * 2 + y) * CI, i * 256 + p * 128
                d_ref[row : row + CI, col : col + 128] = pair.astype(BF)
                for z in range(2):
                    row, col = ((i + z) * 4 + s) * CI, (k * 2 + z) * 128
                    turned[row : row + CI, col : col + 128] = pair
    d_copy = pltpu.make_async_copy(d_ref, d_out, sem.at[0])
    d_copy.start()
    a_ref[...] = turned[...].T.astype(BF)
    a_copy = pltpu.make_async_copy(a_ref, a_out, sem.at[1])
    a_copy.start()
    d_copy.wait()
    a_copy.wait()


def join_b_kernel(f_ref, t_ref, out_ref):
    f = jnp.sum(f_ref[...].astype(F32), axis=0).astype(BF)
    t = jnp.sum(t_ref[...].astype(F32), axis=0).astype(BF)
    for n in range(COLS):
        out_ref[n, 0:FROWS] = f
        out_ref[n, FROWS:] = t


def join_c_kernel(in_ref, out_ref):
    both = jnp.sum(in_ref[...].astype(F32), axis=0).astype(BF)
    for n in range(CHUNKS):
        out_ref[n] = both


def out_kernel(in_ref, sum_ref, taps_ref, bias_ref):
    sum_ref[...] = in_ref[:, 0:FROWS, :].astype(F32).reshape(CHUNKS * FROWS, NX)
    scale = 1.0 / math.sqrt(8 * 64 * NY * NX)
    t = in_ref[:, FROWS:, :].astype(F32).reshape(CHUNKS * TROWS, NX) * scale
    for ij in range(9):
        two = t[ij * CI : ij * CI + CI]
        taps_ref[ij, 0] = two[:, 0:CO]
        taps_ref[ij, 1] = two[:, CO : 2 * CO]
        at, lane = (288 + ij * CI, 0) if ij < 5 else (288 + (ij - 5) * CI, CO)
        taps_ref[ij, 2] = t[at : at + CI, lane : lane + CO]
    bias_ref[...] = t[448:449, CO : 2 * CO]


def exchange(parts, axes):
    return lax.all_to_all(parts, axes, 0, 0)


def join_b(fin, taps):
    sds = jax.ShapeDtypeStruct((COLS, FROWS + TROWS, NX), BF)
    return call(join_b_kernel, sds, [], [VM] * 2, 1 << 20, 1 << 20)(fin, taps)


def join_c(parts):
    sds = jax.ShapeDtypeStruct((CHUNKS, FROWS + TROWS, NX), BF)
    return call(join_c_kernel, sds, [], [VM], 1 << 20, 1 << 20)(parts)


def neighbours(low, high):
    up = [(i, i + 1) for i in range(31)]
    down = [(i + 1, i) for i in range(31)]
    return lax.ppermute(high, SPACE, up), lax.ppermute(low, SPACE, down)


def far(x):
    return pltpu.with_memory_space_constraint(x, pltpu.HBM)


def layer(volumes, kernel, bias, cotangent, finished_grads):
    sds = jax.ShapeDtypeStruct
    x_plane = sds((PADY * CI, NX), BF)
    g_plane = sds((PADY * CO, NX), BF)
    turn = call(
        turn_kernel,
        (pltpu.HBM(x_plane.shape, BF), pltpu.HBM(x_plane.shape, BF)),
        [pltpu.VMEM((CI, 2, NY, NX), BF)]
        + [pltpu.VMEM((NY * CI, NX), F32)] * 2
        + [pltpu.VMEM((PADY * CI, NX), BF)] * 2
        + [DMA((4,)), DMA((2,))],
        [HBM],
        1 << 22,
        3 << 20,
        (HBM, HBM),
    )
    xbuf = pltpu.VMEM((PADY * CI, NX), BF)
    gbuf = pltpu.VMEM((PADY * CO, NX), BF)
    g_out = pltpu.HBM(g_plane.shape, BF)
    forward = call(
        forward_kernel,
        (pltpu.HBM((CO, 2, NY, NX), BF), g_out, g_out),
        [xbuf] * 4
        + [pltpu.VMEM((768, 512), BF)]
        + [pltpu.VMEM((CO, 2, NY, NX), BF)] * 2
        + [gbuf] * 2
        + [pltpu.VMEM((NY * CO, NX), F32)] * 2
        + [DMA((10,)), DMA((6,))],
        [ANY, HBM, HBM, ANY, HBM, pl.BlockSpec(memory_space=pltpu.SMEM), HBM],
        3 << 32,
        8 << 20,
        (HBM, HBM, HBM),
    )
    weight = call(
        weight_kernel,
        sds((512, NX), BF),
        [xbuf] * 4 + [gbuf] * 2 + [pltpu.VMEM((304, 192), F32), DMA((12,))],
        [ANY, HBM, HBM, ANY, HBM, HBM],
        3 << 32,
        5 << 20,
    )
    back = call(
        back_kernel,
        pltpu.HBM((CI, 2, NY, NX), BF),
        [gbuf] * 4
        + [pltpu.VMEM((192, 768), BF), pltpu.VMEM((CI, 2, NY, NX), BF)]
        + [pltpu.VMEM((NY * CI, NX), F32)] * 2
        + [DMA((9,)), DMA((2,))],
        [ANY, HBM, HBM, ANY, HBM],
        3 << 32,
        8 << 20,
        HBM,
    )
    prep = call(
        prep_kernel,
        (pltpu.HBM((768, 512), BF), pltpu.HBM((192, 768), BF), sds((CHUNKS, FROWS, NX), BF)),
        [
            pltpu.VMEM((512, 768), F32),
            pltpu.VMEM((768, 512), BF),
            pltpu.VMEM((192, 768), BF),
            DMA((2,)),
        ],
        [VM] * 2,
        1 << 22,
        3 << 20,
        (HBM, HBM, VM),
    )
    out = call(
        out_kernel,
        (sds((CHUNKS * FROWS, NX), F32), sds((9, 3, CI, CO), F32), sds((1, CO), F32)),
        [],
        [VM],
        1 << 22,
        3 << 20,
    )
    x0, x1 = turn(far(volumes[0]))
    x_low, x_high = neighbours(x0, x1)
    wf, wb, fin = prep(kernel.transpose(0, 1, 2, 4, 3), finished_grads.reshape(2048, NX))
    fin = exchange(fin, PLANE)
    act, g0, g1 = forward(x_low, far(x0), far(x1), x_high, far(wf), bias, far(cotangent[0]))
    g_low, g_high = neighbours(g0, g1)
    taps = weight(x_low, far(x0), far(x1), x_high, far(g0), far(g1))
    taps = exchange(taps.reshape(CHUNKS, TROWS, NX), PLANE)
    joined = join_b(fin, taps)
    joined = exchange(joined, COLUMN)
    joined = join_c(joined)
    joined = exchange(joined, PLANE)
    grad_volumes = back(g_low, far(g0), far(g1), g_high, far(wb))
    summed, grad_taps, grad_bias = out(joined)
    grad_kernel = grad_taps.reshape(3, 3, 3, CI, CO).transpose(0, 1, 2, 4, 3)
    return act[None], grad_volumes[None], grad_kernel, grad_bias.reshape(CO), summed.reshape(-1)


def solution(mesh):
    fine = Mesh(mesh.devices.reshape(2, 4, 8, 2, 2), ("yl", "x", "z", "yh", "c"))
    dp = ("yl", "x")
    slab = P(dp, None, SPACE, None, None)
    return jax.shard_map(
        layer,
        mesh=fine,
        in_specs=(slab, P(), P(), slab, P(dp, SPACE, None)),
        out_specs=(slab, slab, P(), P(), P()),
        check_vma=False,
    )
```

```python
import math

import jax
import jax.numpy as jnp
from jax import lax
from jax.experimental import pallas as pl
from jax.experimental.pallas import tpu as pltpu
from jax.sharding import Mesh, PartitionSpec as P

BF = jnp.bfloat16
F32 = jnp.float32
CI, CO, NY, NX = 32, 64, 48, 128
PADY = NY + 2
PLANE = ("yl", "x", "yh", "c")
COLUMN = "z"
CHUNKS, COLS = 32, 8
FROWS, TROWS = 64, 16
SPACE = ("z", "yh", "c")


def call(body, outs, scratch, specs, flops, nbytes, out_specs=None):
    return pl.pallas_call(
        body,
        out_shape=outs,
        in_specs=specs,
        out_specs=out_specs or jax.tree.map(lambda _: VM, outs),
        scratch_shapes=scratch,
        compiler_params=pltpu.CompilerParams(vmem_limit_bytes=48 << 20),
        cost_estimate=pl.CostEstimate(flops=flops, transcendentals=0, bytes_accessed=nbytes),
    )


VM = pl.BlockSpec(memory_space=pltpu.VMEM)
HBM = pl.BlockSpec(memory_space=pltpu.HBM)
ANY = pl.BlockSpec(memory_space=pl.ANY)
DMA = pltpu.SemaphoreType.DMA


def by_core(copy_pairs, sems):
    core = lax.axis_index("c")
    for n, pairs in enumerate(copy_pairs):
        for side, (src, dst) in enumerate(pairs):

            @pl.when(core == side)
            def _(src=src, dst=dst, n=n):
                pltpu.make_async_copy(src, dst, sems.at[n]).start()

    return [pltpu.make_async_copy(*pairs[0], sems.at[n]) for n, pairs in enumerate(copy_pairs)]


def turn_kernel(x_ref, inner_ref, outer_ref, x, s0, s1, b0, b1, in_sem, out_sem):
    parts = [
        [
            pltpu.make_async_copy(
                x_ref.at[pl.ds(16 * n, 16), z], x.at[pl.ds(16 * n, 16), z], in_sem.at[2 * z + n]
            )
            for n in range(2)
        ]
        for z in range(2)
    ]
    for part in parts[0] + parts[1]:
        part.start()
    for b in (b0, b1):
        b[0:CI, :] = jnp.zeros((CI, NX), BF)
        b[CI * (NY + 1) : CI * PADY, :] = jnp.zeros((CI, NX), BF)
    outs = []
    for z, (s, b) in enumerate(((s0, b0), (s1, b1))):
        for n in range(2):
            parts[z][n].wait()
            for c in range(16 * n, 16 * n + 16):
                s[pl.ds(c, NY, stride=CI), :] = x[c, z].astype(F32)
        b[CI : CI * (NY + 1), :] = s[...].astype(BF)
        first, second = (outer_ref, inner_ref) if z == 0 else (inner_ref, outer_ref)
        outs += by_core([((b, first), (b, second))], out_sem.at[pl.ds(z, 1)])
    for out in outs:
        out.wait()


def shifted_sum(before, middle, after):
    lane = lax.broadcasted_iota(jnp.int32, middle.shape, 1)
    left = jnp.where(lane == 0, 0.0, pltpu.roll(before, 1, 1))
    right = jnp.where(lane == NX - 1, 0.0, pltpu.roll(after, NX - 1, 1))
    return middle + left + right


HALF = NY // 2 + 2


def halves(sources, buffers, width, sems):
    waits = []
    for half, rows in enumerate((pl.ds(0, HALF * width), pl.ds(HALF * width, (PADY - HALF) * width))):
        pairs = [
            tuple((src.at[rows], b.at[rows]) for src in both) for both, b in zip(sources, buffers)
        ]
        waits.append(by_core(pairs, sems.at[pl.ds(half * len(buffers), len(buffers))]))
    return waits


def x_sources(far_inner, far_outer, inner, outer):
    return ((far_outer, far_inner), (outer, inner), (inner, outer), (far_inner, far_outer))


def forward_kernel(*refs):
    p_refs, (a_ref, bias_ref, cot_ref, act_ref, g0_ref, g1_ref) = refs[:4], refs[4:10]
    planes, (a, cot, act, g0, g1, s0, s1, in_sem, act_sem) = refs[10:14], refs[14:]
    a_copy = pltpu.make_async_copy(a_ref, a, in_sem.at[8])
    a_copy.start()
    first, second = halves(x_sources(*p_refs), planes, CI, in_sem)
    cot_copy = pltpu.make_async_copy(cot_ref, cot, in_sem.at[9])
    cot_copy.start()
    for g in (g0, g1):
        g[0:CO, :] = jnp.zeros((CO, NX), BF)
        g[CO * (NY + 1) : CO * PADY, :] = jnp.zeros((CO, NX), BF)

    def conv(q, _):
        sides = []
        for h in range(2):
            start = pl.multiple_of((2 * q + h) * (2 * CI), 2 * CI)
            sides.append(jnp.concatenate([p[pl.ds(start, 4 * CI), :] for p in planes], axis=0))
        rhs = jnp.concatenate(sides, axis=1)
        r = jnp.dot(a[...], rhs, preferred_element_type=F32)
        for h in range(2):
            rr = r[:, NX * h : NX * (h + 1)]
            y = shifted_sum(rr[0:256], rr[256:512], rr[512:768])
            at = pl.multiple_of((2 * q + h) * 128, 128)
            s0[pl.ds(at, 128), :] = y[0:128]
            s1[pl.ds(at, 128), :] = y[128:256]
        return 0

    a_copy.wait()
    for part, lo in ((first, 0), (second, 6)):
        for copy in part:
            copy.wait()
        lax.fori_loop(lo, lo + 6, conv, 0)
    cot_copy.wait()

    def point(o, _):
        b = bias_ref[o]
        for z, s in ((0, s0), (1, s1)):
            v = s[pl.ds(o, NY, stride=CO), :] + b
            sig = 0.5 + 0.5 * jnp.tanh(0.5 * jnp.abs(v))
            soft = jnp.maximum(v, 0.0) - jnp.log(sig)
            act[o, z] = (0.3 * v + 0.7 * soft).astype(BF)
            slope = 0.3 + 0.7 * jnp.where(v >= 0, sig, 1.0 - sig)
            s[pl.ds(o, NY, stride=CO), :] = cot[o, z].astype(F32) * slope
        return 0

    outs = []
    for n in range(4):
        lax.fori_loop(16 * n, 16 * n + 16, point, 0, unroll=2)
        some = pl.ds(16 * n, 16)
        outs.append(pltpu.make_async_copy(act.at[some], act_ref.at[some], act_sem.at[n]))
        outs[-1].start()
    for n, (g_ref, g, s) in enumerate(((g0_ref, g0, s0), (g1_ref, g1, s1))):
        g[CO : CO * (NY + 1), :] = s[...].astype(BF)
        outs.append(pltpu.make_async_copy(g, g_ref, act_sem.at[4 + n]))
        outs[-1].start()
    for out in outs:
        out.wait()


def weight_kernel(*refs):
    p_refs, g_refs, out_ref = refs[:4], refs[4:6], refs[6]
    planes, gs_buf, acc, sems = refs[7:11], refs[11:13], refs[13], refs[14]
    first, second = halves(x_sources(*p_refs), planes, CI, sems)
    g_first, g_second = halves([(g, g) for g in g_refs], gs_buf, CO, sems.at[pl.ds(8, 4)])
    acc[...] = jnp.zeros_like(acc)
    lane = lax.broadcasted_iota(jnp.int32, (CO, NX), 1)

    def row(y, _):
        gs, xs = [], []
        ystart = pl.multiple_of(y * CI, CI)
        gstart = pl.multiple_of((y + 1) * CO, CO)
        for z, g in enumerate(gs_buf):
            mid = g[pl.ds(gstart, CO), :]
            wide = mid.astype(F32)
            before = jnp.where(lane == NX - 1, 0.0, pltpu.roll(wide, NX - 1, 1)).astype(BF)
            after = jnp.where(lane == 0, 0.0, pltpu.roll(wide, 1, 1)).astype(BF)
            gs.append(jnp.concatenate([before, mid, after], axis=0))
            xs.append(
                jnp.concatenate(
                    [planes[z + i][pl.ds(ystart, 3 * CI), :] for i in range(3)]
                    + [jnp.ones((16, NX), BF)],
                    axis=0,
                )
            )
        acc[...] += lax.dot_general(
            jnp.concatenate(xs, axis=1),
            jnp.concatenate(gs, axis=1),
            (((1,), (1,)), ((), ())),
            preferred_element_type=F32,
        )
        return 0

    for part, lo in ((first + g_first, 0), (second + g_second, 24)):
        for copy in part:
            copy.wait()
        lax.fori_loop(lo, lo + 24, row, 0, unroll=2)
    out_ref[0:288, :] = acc[0:288, 0:128].astype(BF)
    side = acc[0:288, 128:192]
    tail = jnp.concatenate([side[160:288], jnp.zeros((32, CO), F32)], axis=0)
    out_ref[288:448, :] = jnp.concatenate([side[0:160], tail], axis=1).astype(BF)
    out_ref[448:464, :] = acc[288:304, 0:128].astype(BF)
    out_ref[464:512, :] = jnp.zeros((48, NX), BF)


def back_kernel(g0_ref, g1_ref, d_ref, own0_ref, own1_ref, inner_ref, outer_ref, *rest):
    g0, g1, d, s0, s1, low, high, sems, out_sem = rest
    d_copy = pltpu.make_async_copy(d_ref, d, sems.at[4])
    d_copy.start()
    first, second = halves([(g0_ref, g0_ref), (g1_ref, g1_ref)], (g0, g1), CO, sems)

    def conv(q, _):
        r = []
        for g in (g0, g1):
            sides = [
                g[pl.ds(pl.multiple_of((2 * q + h) * (2 * CO), 2 * CO), 4 * CO), :] for h in range(2)
            ]
            r.append(jnp.dot(d[...], jnp.concatenate(sides, axis=1), preferred_element_type=F32))
        volumes = (r[0][0:192], r[0][192:384] + r[1][0:192], r[0][384:576] + r[1][192:384], r[1][384:576])
        for v, s in zip(volumes, (low, s0, s1, high)):
            for h in range(2):
                rr = v[:, NX * h : NX * (h + 1)]
                at = pl.multiple_of((2 * q + h) * (2 * CI), 2 * CI)
                y = shifted_sum(rr[128:192], rr[64:128], rr[0:64])
                s[pl.ds(at, 2 * CI), :] = y.astype(s.dtype)
        return 0

    d_copy.wait()
    for part, lo in ((first, 0), (second, 6)):
        for copy in part:
            copy.wait()
        lax.fori_loop(lo, lo + 6, conv, 0)
    outs = by_core(
        [((high, inner_ref), (low, inner_ref)), ((low, outer_ref), (high, outer_ref))],
        out_sem.at[pl.ds(0, 2)],
    )
    for n, (s, own) in enumerate(((s0, own0_ref), (s1, own1_ref))):
        outs.append(pltpu.make_async_copy(s, own, out_sem.at[2 + n]))
        outs[-1].start()
    for out in outs:
        out.wait()


def finish_kernel(own0_ref, own1_ref, inner_ref, outer_ref, out_ref, s0, s1, e0, e1, buf, sems, out_sem):
    loads = by_core(
        [((outer_ref, e0), (inner_ref, e0)), ((inner_ref, e1), (outer_ref, e1))], sems.at[pl.ds(0, 2)]
    )
    for n, (own, s) in enumerate(((own0_ref, s0), (own1_ref, s1))):
        loads.append(pltpu.make_async_copy(own, s, sems.at[2 + n]))
        loads[-1].start()
    for load in loads:
        load.wait()
    for s, e in ((s0, e0), (s1, e1)):
        s[...] += e[...].astype(F32)

    def gather(c, _):
        for z, s in ((0, s0), (1, s1)):
            buf[c, z] = s[pl.ds(c, NY, stride=CI), :].astype(BF)
        return 0

    outs = []
    for n in range(2):
        lax.fori_loop(16 * n, 16 * n + 16, gather, 0, unroll=4)
        some = pl.ds(16 * n, 16)
        outs.append(pltpu.make_async_copy(buf.at[some], out_ref.at[some], out_sem.at[n]))
        outs[-1].start()
    for out in outs:
        out.wait()


def prep_kernel(w_hbm, f_hbm, a_out, d_out, out_ref, turned, a_ref, d_ref, w_ref, f_ref, sem):
    w_copy = pltpu.make_async_copy(w_hbm, w_ref, sem.at[2])
    w_copy.start()
    f_copies = [
        pltpu.make_async_copy(f_hbm.at[pl.ds(512 * n, 512)], f_ref.at[pl.ds(512 * n, 512)], sem.at[3 + n])
        for n in range(4)
    ]
    for copy in f_copies:
        copy.start()
    w_copy.wait()
    for z, hole in ((0, 3), (1, 0)):
        for k in range(3):
            col = (k * 2 + z) * 128
            turned[hole * 128 : hole * 128 + 128, col : col + 128] = jnp.zeros((128, 128), F32)
    for i in range(3):
        for k in range(3):
            w = [w_ref[i, j, k].astype(F32) for j in range(3)]
            none = jnp.zeros((CI, CO), F32)
            for s in range(4):
                pair = jnp.concatenate([w[s] if s < 3 else none, w[s - 1] if s else none], axis=1)
                y, p = ((0, 1), (1, 1), (0, 0), (1, 0))[s]
                row, col = i * 192 + (k * 2 + y) * CI, p * 128
                d_ref[row : row + CI, col : col + 128] = pair.astype(BF)
                for z in range(2):
                    row, col = ((i + z) * 4 + s) * CI, (k * 2 + z) * 128
                    turned[row : row + CI, col : col + 128] = pair
    d_copy = pltpu.make_async_copy(d_ref, d_out, sem.at[0])
    d_copy.start()
    a_ref[...] = turned[...].T.astype(BF)
    a_copy = pltpu.make_async_copy(a_ref, a_out, sem.at[1])
    a_copy.start()
    for n, copy in enumerate(f_copies):
        copy.wait()
        part = f_ref[512 * n : 512 * n + 512, :]
        out_ref[8 * n : 8 * n + 8] = part.reshape(8, FROWS, NX).astype(BF)
    d_copy.wait()
    a_copy.wait()


def join_b_kernel(f_ref, t_ref, out_ref):
    f = jnp.sum(f_ref[...].astype(F32), axis=0).astype(BF)
    t = jnp.sum(t_ref[...].astype(F32), axis=0).astype(BF)
    for n in range(COLS):
        out_ref[n, 0:FROWS] = f
        out_ref[n, FROWS:] = t


def join_c_kernel(in_ref, out_ref):
    both = jnp.sum(in_ref[...].astype(F32), axis=0).astype(BF)
    for n in range(CHUNKS):
        out_ref[n] = both


def out_kernel(in_ref, sum_ref, taps_ref, bias_ref):
    sum_ref[...] = in_ref[:, 0:FROWS, :].astype(F32).reshape(CHUNKS * FROWS, NX)
    scale = 1.0 / math.sqrt(8 * 64 * NY * NX)
    t = in_ref[:, FROWS:, :].astype(F32).reshape(CHUNKS * TROWS, NX) * scale
    for ij in range(9):
        two = t[ij * CI : ij * CI + CI]
        taps_ref[ij, 0] = two[:, 0:CO]
        taps_ref[ij, 1] = two[:, CO : 2 * CO]
        at, lane = (288 + ij * CI, 0) if ij < 5 else (288 + (ij - 5) * CI, CO)
        taps_ref[ij, 2] = t[at : at + CI, lane : lane + CO]
    bias_ref[...] = t[448:449, CO : 2 * CO]


def exchange(parts, axes):
    return lax.all_to_all(parts, axes, 0, 0)


def join_b(fin, taps):
    sds = jax.ShapeDtypeStruct((COLS, FROWS + TROWS, NX), BF)
    return call(join_b_kernel, sds, [], [VM] * 2, 1 << 20, 1 << 20)(fin, taps)


def join_c(parts):
    sds = jax.ShapeDtypeStruct((CHUNKS, FROWS + TROWS, NX), BF)
    return call(join_c_kernel, sds, [], [VM], 1 << 20, 1 << 20)(parts)


def swap(inner, outer):
    on_chip = [(i, i ^ 1) for i in range(32)]
    off_chip = [(i, i + 1) for i in range(1, 31, 2)] + [(i + 1, i) for i in range(1, 31, 2)]
    return lax.ppermute(inner, SPACE, on_chip), lax.ppermute(outer, SPACE, off_chip)


def far(x):
    return pltpu.with_memory_space_constraint(x, pltpu.HBM)


def layer(volumes, kernel, bias, cotangent, finished_grads):
    sds = jax.ShapeDtypeStruct
    x_plane = sds((PADY * CI, NX), BF)
    g_plane = sds((PADY * CO, NX), BF)
    turn = call(
        turn_kernel,
        (pltpu.HBM(x_plane.shape, BF), pltpu.HBM(x_plane.shape, BF)),
        [pltpu.VMEM((CI, 2, NY, NX), BF)]
        + [pltpu.VMEM((NY * CI, NX), F32)] * 2
        + [pltpu.VMEM((PADY * CI, NX), BF)] * 2
        + [DMA((4,)), DMA((2,))],
        [HBM],
        1 << 22,
        3 << 20,
        (HBM, HBM),
    )
    xbuf = pltpu.VMEM((PADY * CI, NX), BF)
    gbuf = pltpu.VMEM((PADY * CO, NX), BF)
    g_out = pltpu.HBM(g_plane.shape, BF)
    forward = call(
        forward_kernel,
        (pltpu.HBM((CO, 2, NY, NX), BF), g_out, g_out),
        [xbuf] * 4
        + [pltpu.VMEM((768, 512), BF)]
        + [pltpu.VMEM((CO, 2, NY, NX), BF)] * 2
        + [gbuf] * 2
        + [pltpu.VMEM((NY * CO, NX), F32)] * 2
        + [DMA((10,)), DMA((6,))],
        [ANY, ANY, HBM, HBM, HBM, pl.BlockSpec(memory_space=pltpu.SMEM), HBM],
        3 << 32,
        8 << 20,
        (HBM, HBM, HBM),
    )
    weight = call(
        weight_kernel,
        sds((512, NX), BF),
        [xbuf] * 4 + [gbuf] * 2 + [pltpu.VMEM((304, 192), F32), DMA((12,))],
        [ANY, ANY, HBM, HBM, HBM, HBM],
        3 << 32,
        5 << 20,
    )
    edge = (NY * CI, NX)
    back = call(
        back_kernel,
        (pltpu.HBM(edge, F32), pltpu.HBM(edge, F32), pltpu.HBM(edge, BF), pltpu.HBM(edge, BF)),
        [gbuf] * 2
        + [pltpu.VMEM((576, 256), BF)]
        + [pltpu.VMEM(edge, F32)] * 2
        + [pltpu.VMEM(edge, BF)] * 2
        + [DMA((5,)), DMA((4,))],
        [HBM] * 3,
        3 << 32,
        8 << 20,
        (HBM,) * 4,
    )
    finish = call(
        finish_kernel,
        pltpu.HBM((CI, 2, NY, NX), BF),
        [pltpu.VMEM(edge, F32)] * 2
        + [pltpu.VMEM(edge, BF)] * 2
        + [pltpu.VMEM((CI, 2, NY, NX), BF), DMA((4,)), DMA((2,))],
        [HBM, HBM, ANY, ANY],
        1 << 28,
        4 << 20,
        HBM,
    )
    prep = call(
        prep_kernel,
        (pltpu.HBM((768, 512), BF), pltpu.HBM((576, 256), BF), sds((CHUNKS, FROWS, NX), BF)),
        [
            pltpu.VMEM((512, 768), F32),
            pltpu.VMEM((768, 512), BF),
            pltpu.VMEM((576, 256), BF),
            pltpu.VMEM((3, 3, 3, CI, CO), BF),
            pltpu.VMEM((2048, NX), F32),
            DMA((7,)),
        ],
        [HBM] * 2,
        1 << 22,
        3 << 20,
        (HBM, HBM, VM),
    )
    out = call(
        out_kernel,
        (sds((CHUNKS * FROWS, NX), F32), sds((9, 3, CI, CO), F32), sds((1, CO), F32)),
        [],
        [VM],
        1 << 22,
        3 << 20,
    )
    inner, outer = turn(far(volumes[0]))
    far_inner, far_outer = swap(inner, outer)
    wf, wb, fin = prep(far(kernel.transpose(0, 1, 2, 4, 3)), far(finished_grads.reshape(2048, NX)))
    fin = exchange(fin, PLANE)
    x = (far_inner, far_outer, far(inner), far(outer))
    act, g0, g1 = forward(*x, far(wf), bias, far(cotangent[0]))
    taps = weight(*x, far(g0), far(g1))
    taps = exchange(taps.reshape(CHUNKS, TROWS, NX), PLANE)
    own0, own1, inner, outer = back(far(g0), far(g1), far(wb))
    far_inner, far_outer = swap(inner, outer)
    joined = join_b(fin, taps)
    joined = exchange(joined, COLUMN)
    joined = join_c(joined)
    joined = exchange(joined, PLANE)
    grad_volumes = finish(far(own0), far(own1), far_inner, far_outer)
    summed, grad_taps, grad_bias = out(joined)
    grad_kernel = grad_taps.reshape(3, 3, 3, CI, CO).transpose(0, 1, 2, 4, 3)
    return act[None], grad_volumes[None], grad_kernel, grad_bias.reshape(CO), summed.reshape(-1)


def solution(mesh):
    fine = Mesh(mesh.devices.reshape(2, 4, 8, 2, 2), ("yl", "x", "z", "yh", "c"))
    dp = ("yl", "x")
    slab = P(dp, None, SPACE, None, None)
    return jax.shard_map(
        layer,
        mesh=fine,
        in_specs=(slab, P(), P(), slab, P(dp, SPACE, None)),
        out_specs=(slab, slab, P(), P(), P()),
        check_vma=False,
    )
```

```python
import math

import jax
import jax.numpy as jnp
from jax import lax
from jax.experimental import pallas as pl
from jax.experimental.pallas import tpu as pltpu
from jax.sharding import Mesh, PartitionSpec as P

BF = jnp.bfloat16
F32 = jnp.float32
CI, CO, NY, NX = 32, 64, 48, 128
PADY = NY + 2
PLANE = ("yl", "x", "yh", "c")
COLUMN = "z"
CHUNKS, COLS = 32, 8
FROWS, TROWS = 64, 16
SPACE = ("z", "yh", "c")


def call(body, outs, scratch, specs, flops, nbytes, out_specs=None):
    return pl.pallas_call(
        body,
        out_shape=outs,
        in_specs=specs,
        out_specs=out_specs or jax.tree.map(lambda _: VM, outs),
        scratch_shapes=scratch,
        compiler_params=pltpu.CompilerParams(vmem_limit_bytes=48 << 20),
        cost_estimate=pl.CostEstimate(flops=flops, transcendentals=0, bytes_accessed=nbytes),
    )


VM = pl.BlockSpec(memory_space=pltpu.VMEM)
HBM = pl.BlockSpec(memory_space=pltpu.HBM)
ANY = pl.BlockSpec(memory_space=pl.ANY)
DMA = pltpu.SemaphoreType.DMA


def row_of(y, block, blocks):
    return pl.multiple_of(((y // 8) * blocks + block) * 64 + (y % 8) * 8, 8)


def by_core(copy_pairs, sems):
    core = lax.axis_index("c")
    for n, pairs in enumerate(copy_pairs):
        for side, (src, dst) in enumerate(pairs):

            @pl.when(core == side)
            def _(src=src, dst=dst, n=n):
                pltpu.make_async_copy(src, dst, sems.at[n]).start()

    return [pltpu.make_async_copy(*pairs[0], sems.at[n]) for n, pairs in enumerate(copy_pairs)]


def turn_kernel(x_ref, inner_ref, outer_ref, x, s0, s1, b0, b1, in_sem, out_sem):
    parts = [
        [
            pltpu.make_async_copy(
                x_ref.at[pl.ds(16 * n, 16), z], x.at[pl.ds(16 * n, 16), z], in_sem.at[2 * z + n]
            )
            for n in range(2)
        ]
        for z in range(2)
    ]
    for part in parts[0] + parts[1]:
        part.start()
    for b in (b0, b1):
        b[0:CI, :] = jnp.zeros((CI, NX), BF)
        b[CI * (NY + 1) : CI * PADY, :] = jnp.zeros((CI, NX), BF)
    outs = []
    for z, (s, b) in enumerate(((s0, b0), (s1, b1))):
        for n in range(2):
            parts[z][n].wait()
            for c in range(16 * n, 16 * n + 16):
                v = x[c, z].astype(F32)
                for m in range(NY // 8):
                    s[pl.ds((m * 4 + c // 8) * 64 + c % 8, 8, stride=8), :] = v[8 * m : 8 * m + 8]
        for y in range(NY):
            v = [s[pl.ds(((y // 8) * 4 + m) * 64 + (y % 8) * 8, 8), :] for m in range(4)]
            b[CI * (y + 1) : CI * (y + 2), :] = jnp.concatenate(v, axis=0).astype(BF)
        first, second = (outer_ref, inner_ref) if z == 0 else (inner_ref, outer_ref)
        outs += by_core([((b, first), (b, second))], out_sem.at[pl.ds(z, 1)])
    for out in outs:
        out.wait()


def shifted_sum(before, middle, after):
    lane = lax.broadcasted_iota(jnp.int32, middle.shape, 1)
    left = jnp.where(lane == 0, 0.0, pltpu.roll(before, 1, 1))
    right = jnp.where(lane == NX - 1, 0.0, pltpu.roll(after, NX - 1, 1))
    return middle + left + right


HALF = NY // 2 + 2


def halves(sources, buffers, width, sems):
    waits = []
    for half, rows in enumerate((pl.ds(0, HALF * width), pl.ds(HALF * width, (PADY - HALF) * width))):
        pairs = [
            tuple((src.at[rows], b.at[rows]) for src in both) for both, b in zip(sources, buffers)
        ]
        waits.append(by_core(pairs, sems.at[pl.ds(half * len(buffers), len(buffers))]))
    return waits


def x_sources(far_inner, far_outer, inner, outer):
    return ((far_outer, far_inner), (outer, inner), (inner, outer), (far_inner, far_outer))


def forward_kernel(*refs):
    p_refs, (a_ref, bias_ref, cot_ref, act_ref, g0_ref, g1_ref) = refs[:4], refs[4:10]
    planes, (a, cot, act, g0, g1, s0, s1, in_sem, act_sem) = refs[10:14], refs[14:]
    a_copy = pltpu.make_async_copy(a_ref, a, in_sem.at[8])
    a_copy.start()
    first, second = halves(x_sources(*p_refs), planes, CI, in_sem)
    cot_copy = pltpu.make_async_copy(cot_ref, cot, in_sem.at[9])
    cot_copy.start()
    for g in (g0, g1):
        g[0:CO, :] = jnp.zeros((CO, NX), BF)
        g[CO * (NY + 1) : CO * PADY, :] = jnp.zeros((CO, NX), BF)

    def conv(q, _):
        sides = []
        for h in range(2):
            start = pl.multiple_of((2 * q + h) * (2 * CI), 2 * CI)
            sides.append(jnp.concatenate([p[pl.ds(start, 4 * CI), :] for p in planes], axis=0))
        rhs = jnp.concatenate(sides, axis=1)
        r = jnp.dot(a[...], rhs, preferred_element_type=F32)
        for h in range(2):
            rr = r[:, NX * h : NX * (h + 1)]
            y = shifted_sum(rr[0:256], rr[256:512], rr[512:768])
            for z, s in enumerate((s0, s1)):
                for p in range(2):
                    for m in range(8):
                        at = row_of(4 * q + 2 * h + p, m, 8)
                        s[pl.ds(at, 8), :] = y[128 * z + 64 * p + 8 * m : 128 * z + 64 * p + 8 * m + 8]
        return 0

    a_copy.wait()
    for part, lo in ((first, 0), (second, 6)):
        for copy in part:
            copy.wait()
        lax.fori_loop(lo, lo + 6, conv, 0, unroll=2)
    cot_copy.wait()

    def point(m, _):
        for n in range(8):
            o = m * 8 + n
            b = bias_ref[o]
            for z, s in ((0, s0), (1, s1)):
                for y in range(0, NY // 8, 2):
                    rows = [pl.ds(((y + u) * 8 + m) * 64 + n, 8, stride=8) for u in range(2)]
                    v = jnp.concatenate([s[r, :] for r in rows], axis=0) + b
                    t = jnp.tanh(0.5 * v)
                    soft = 0.7 * jnp.log(0.5 + 0.5 * jnp.abs(t))
                    act[o, z, 8 * y : 8 * y + 16, :] = (jnp.maximum(v, 0.3 * v) - soft).astype(BF)
                    grad = cot[o, z, 8 * y : 8 * y + 16, :].astype(F32) * (0.65 + 0.35 * t)
                    s[rows[0], :] = grad[0:8]
                    s[rows[1], :] = grad[8:16]
        some = pl.ds(8 * m, 8)
        pltpu.make_async_copy(act.at[some], act_ref.at[some], act_sem.at[m]).start()
        return 0

    lax.fori_loop(0, 8, point, 0)
    outs = []
    for n in range(8):
        some = pl.ds(8 * n, 8)
        outs.append(pltpu.make_async_copy(act.at[some], act_ref.at[some], act_sem.at[n]))
    for n, (g_ref, g, s) in enumerate(((g0_ref, g0, s0), (g1_ref, g1, s1))):

        def rows_of(t, _, g=g, s=s):
            for y in range(8):
                v = [s[pl.ds((t * 8 + m) * 64 + y * 8, 8), :] for m in range(8)]
                at = pl.multiple_of((t * 8 + y + 1) * CO, CO)
                g[pl.ds(at, CO), :] = jnp.concatenate(v, axis=0).astype(BF)
            return 0

        lax.fori_loop(0, NY // 8, rows_of, 0)
        outs.append(pltpu.make_async_copy(g, g_ref, act_sem.at[8 + n]))
        outs[-1].start()
    for out in outs:
        out.wait()


def weight_kernel(*refs):
    p_refs, g_refs, out_ref = refs[:4], refs[4:6], refs[6]
    planes, gs_buf, acc, sems = refs[7:11], refs[11:13], refs[13], refs[14]
    first, second = halves(x_sources(*p_refs), planes, CI, sems)
    g_first, g_second = halves([(g, g) for g in g_refs], gs_buf, CO, sems.at[pl.ds(8, 4)])
    acc[...] = jnp.zeros_like(acc)
    lane = lax.broadcasted_iota(jnp.int32, (CO, NX), 1)

    def rows(q, _):
        gs, xs = [], []
        for y in range(4):
            ystart = pl.multiple_of((4 * q + y) * CI, CI)
            gstart = pl.multiple_of((4 * q + y + 1) * CO, CO)
            for z, g in enumerate(gs_buf):
                mid = g[pl.ds(gstart, CO), :]
                wide = mid.astype(F32)
                before = jnp.where(lane == NX - 1, 0.0, pltpu.roll(wide, NX - 1, 1)).astype(BF)
                after = jnp.where(lane == 0, 0.0, pltpu.roll(wide, 1, 1)).astype(BF)
                gs.append(jnp.concatenate([before, mid, after], axis=0))
                xs.append(
                    jnp.concatenate(
                        [planes[z + i][pl.ds(ystart, 3 * CI), :] for i in range(3)]
                        + [jnp.ones((16, NX), BF)],
                        axis=0,
                    )
                )
        acc[...] += lax.dot_general(
            jnp.concatenate(xs, axis=1),
            jnp.concatenate(gs, axis=1),
            (((1,), (1,)), ((), ())),
            preferred_element_type=F32,
        )
        return 0

    for part, lo in ((first + g_first, 0), (second + g_second, 24)):
        for copy in part:
            copy.wait()
        lax.fori_loop(lo // 4, lo // 4 + 6, rows, 0)
    out_ref[0:288, :] = acc[0:288, 0:128].astype(BF)
    side = acc[0:288, 128:192]
    tail = jnp.concatenate([side[160:288], jnp.zeros((32, CO), F32)], axis=0)
    out_ref[288:448, :] = jnp.concatenate([side[0:160], tail], axis=1).astype(BF)
    out_ref[448:464, :] = acc[288:304, 0:128].astype(BF)
    out_ref[464:512, :] = jnp.zeros((48, NX), BF)


def back_kernel(g0_ref, g1_ref, d_ref, own0_ref, own1_ref, inner_ref, outer_ref, *rest):
    g0, g1, d, s0, s1, low, high, sems, out_sem = rest
    d_copy = pltpu.make_async_copy(d_ref, d, sems.at[4])
    d_copy.start()
    first, second = halves([(g0_ref, g0_ref), (g1_ref, g1_ref)], (g0, g1), CO, sems)

    def conv(q, _):
        r = []
        for g in (g0, g1):
            sides = [
                g[pl.ds(pl.multiple_of((2 * q + h) * (2 * CO), 2 * CO), 4 * CO), :] for h in range(2)
            ]
            r.append(jnp.dot(d[...], jnp.concatenate(sides, axis=1), preferred_element_type=F32))
        volumes = (r[0][0:192], r[0][192:384] + r[1][0:192], r[0][384:576] + r[1][192:384], r[1][384:576])
        for v, s in zip(volumes, (low, s0, s1, high)):
            for h in range(2):
                rr = v[:, NX * h : NX * (h + 1)]
                y = shifted_sum(rr[128:192], rr[64:128], rr[0:64])
                if s.dtype == BF:
                    at = pl.multiple_of((2 * q + h) * (2 * CI), 2 * CI)
                    s[pl.ds(at, 2 * CI), :] = y.astype(BF)
                    continue
                for p in range(2):
                    for m in range(4):
                        at = row_of(4 * q + 2 * h + p, m, 4)
                        s[pl.ds(at, 8), :] = y[32 * p + 8 * m : 32 * p + 8 * m + 8]
        return 0

    d_copy.wait()
    for part, lo in ((first, 0), (second, 6)):
        for copy in part:
            copy.wait()
        lax.fori_loop(lo, lo + 6, conv, 0, unroll=2)
    outs = by_core(
        [((high, inner_ref), (low, inner_ref)), ((low, outer_ref), (high, outer_ref))],
        out_sem.at[pl.ds(0, 2)],
    )
    for n, (s, own) in enumerate(((s0, own0_ref), (s1, own1_ref))):
        outs.append(pltpu.make_async_copy(s, own, out_sem.at[2 + n]))
        outs[-1].start()
    for out in outs:
        out.wait()


def finish_kernel(own0_ref, own1_ref, inner_ref, outer_ref, out_ref, s0, s1, e0, e1, buf, sems, out_sem):
    loads = by_core(
        [((outer_ref, e0), (inner_ref, e0)), ((inner_ref, e1), (outer_ref, e1))], sems.at[pl.ds(0, 2)]
    )
    for n, (own, s) in enumerate(((own0_ref, s0), (own1_ref, s1))):
        loads.append(pltpu.make_async_copy(own, s, sems.at[2 + n]))
        loads[-1].start()
    for load in loads:
        load.wait()

    def add(t, _):
        for s, e in ((s0, e0), (s1, e1)):
            for y in range(8):
                v = e[pl.ds(pl.multiple_of((t * 8 + y) * CI, CI), CI), :].astype(F32)
                for m in range(4):
                    at = pl.ds((t * 4 + m) * 64 + y * 8, 8)
                    s[at, :] += v[8 * m : 8 * m + 8]
        return 0

    lax.fori_loop(0, NY // 8, add, 0)

    def gather(m, _):
        for n in range(8):
            for z, s in ((0, s0), (1, s1)):
                v = [s[pl.ds((t * 4 + m) * 64 + n, 8, stride=8), :] for t in range(NY // 8)]
                buf[m * 8 + n, z] = jnp.concatenate(v, axis=0).astype(BF)
        some = pl.ds(8 * m, 8)
        pltpu.make_async_copy(buf.at[some], out_ref.at[some], out_sem.at[m]).start()
        return 0

    lax.fori_loop(0, 4, gather, 0)
    for n in range(4):
        some = pl.ds(8 * n, 8)
        pltpu.make_async_copy(buf.at[some], out_ref.at[some], out_sem.at[n]).wait()


def prep_kernel(w_hbm, f_hbm, a_out, d_out, out_ref, turned, a_ref, d_ref, w_ref, f_ref, sem):
    w_copy = pltpu.make_async_copy(w_hbm, w_ref, sem.at[2])
    w_copy.start()
    f_copies = [
        pltpu.make_async_copy(f_hbm.at[pl.ds(512 * n, 512)], f_ref.at[pl.ds(512 * n, 512)], sem.at[3 + n])
        for n in range(4)
    ]
    for copy in f_copies:
        copy.start()
    w_copy.wait()
    for z, hole in ((0, 3), (1, 0)):
        for k in range(3):
            col = (k * 2 + z) * 128
            turned[hole * 128 : hole * 128 + 128, col : col + 128] = jnp.zeros((128, 128), F32)
    for i in range(3):
        for k in range(3):
            w = [w_ref[i, j, k].astype(F32) for j in range(3)]
            none = jnp.zeros((CI, CO), F32)
            for s in range(4):
                pair = jnp.concatenate([w[s] if s < 3 else none, w[s - 1] if s else none], axis=1)
                y, p = ((0, 1), (1, 1), (0, 0), (1, 0))[s]
                row, col = i * 192 + (k * 2 + y) * CI, p * 128
                d_ref[row : row + CI, col : col + 128] = pair.astype(BF)
                for z in range(2):
                    row, col = ((i + z) * 4 + s) * CI, (k * 2 + z) * 128
                    turned[row : row + CI, col : col + 128] = pair
    d_copy = pltpu.make_async_copy(d_ref, d_out, sem.at[0])
    d_copy.start()
    a_ref[...] = turned[...].T.astype(BF)
    a_copy = pltpu.make_async_copy(a_ref, a_out, sem.at[1])
    a_copy.start()
    for n, copy in enumerate(f_copies):
        copy.wait()
        part = f_ref[512 * n : 512 * n + 512, :]
        out_ref[8 * n : 8 * n + 8] = part.reshape(8, FROWS, NX).astype(BF)
    d_copy.wait()
    a_copy.wait()


def join_b_kernel(f_ref, t_ref, out_ref):
    f = jnp.sum(f_ref[...].astype(F32), axis=0).astype(BF)
    t = jnp.sum(t_ref[...].astype(F32), axis=0).astype(BF)
    for n in range(COLS):
        out_ref[n, 0:FROWS] = f
        out_ref[n, FROWS:] = t


def join_c_kernel(in_ref, out_ref):
    both = jnp.sum(in_ref[...].astype(F32), axis=0).astype(BF)
    for n in range(CHUNKS):
        out_ref[n] = both


def out_kernel(in_ref, sum_ref, taps_ref, bias_ref):
    sum_ref[...] = in_ref[:, 0:FROWS, :].astype(F32).reshape(CHUNKS * FROWS, NX)
    scale = 1.0 / math.sqrt(8 * 64 * NY * NX)
    t = in_ref[:, FROWS:, :].astype(F32).reshape(CHUNKS * TROWS, NX) * scale
    for ij in range(9):
        two = t[ij * CI : ij * CI + CI]
        taps_ref[ij, 0] = two[:, 0:CO]
        taps_ref[ij, 1] = two[:, CO : 2 * CO]
        at, lane = (288 + ij * CI, 0) if ij < 5 else (288 + (ij - 5) * CI, CO)
        taps_ref[ij, 2] = t[at : at + CI, lane : lane + CO]
    bias_ref[...] = t[448:449, CO : 2 * CO]


def exchange(parts, axes):
    return lax.all_to_all(parts, axes, 0, 0)


def join_b(fin, taps):
    sds = jax.ShapeDtypeStruct((COLS, FROWS + TROWS, NX), BF)
    return call(join_b_kernel, sds, [], [VM] * 2, 1 << 20, 1 << 20)(fin, taps)


def join_c(parts):
    sds = jax.ShapeDtypeStruct((CHUNKS, FROWS + TROWS, NX), BF)
    return call(join_c_kernel, sds, [], [VM], 1 << 20, 1 << 20)(parts)


def swap(inner, outer):
    on_chip = [(i, i ^ 1) for i in range(32)]
    off_chip = [(i, i + 1) for i in range(1, 31, 2)] + [(i + 1, i) for i in range(1, 31, 2)]
    return lax.ppermute(inner, SPACE, on_chip), lax.ppermute(outer, SPACE, off_chip)


def far(x):
    return pltpu.with_memory_space_constraint(x, pltpu.HBM)


def layer(volumes, kernel, bias, cotangent, finished_grads):
    sds = jax.ShapeDtypeStruct
    x_plane = sds((PADY * CI, NX), BF)
    g_plane = sds((PADY * CO, NX), BF)
    turn = call(
        turn_kernel,
        (pltpu.HBM(x_plane.shape, BF), pltpu.HBM(x_plane.shape, BF)),
        [pltpu.VMEM((CI, 2, NY, NX), BF)]
        + [pltpu.VMEM((NY * CI, NX), F32)] * 2
        + [pltpu.VMEM((PADY * CI, NX), BF)] * 2
        + [DMA((4,)), DMA((2,))],
        [HBM],
        1 << 22,
        3 << 20,
        (HBM, HBM),
    )
    xbuf = pltpu.VMEM((PADY * CI, NX), BF)
    gbuf = pltpu.VMEM((PADY * CO, NX), BF)
    g_out = pltpu.HBM(g_plane.shape, BF)
    forward = call(
        forward_kernel,
        (pltpu.HBM((CO, 2, NY, NX), BF), g_out, g_out),
        [xbuf] * 4
        + [pltpu.VMEM((768, 512), BF)]
        + [pltpu.VMEM((CO, 2, NY, NX), BF)] * 2
        + [gbuf] * 2
        + [pltpu.VMEM((NY * CO, NX), F32)] * 2
        + [DMA((10,)), DMA((10,))],
        [ANY, ANY, HBM, HBM, HBM, pl.BlockSpec(memory_space=pltpu.SMEM), HBM],
        3 << 32,
        8 << 20,
        (HBM, HBM, HBM),
    )
    weight = call(
        weight_kernel,
        sds((512, NX), BF),
        [xbuf] * 4 + [gbuf] * 2 + [pltpu.VMEM((304, 192), F32), DMA((12,))],
        [ANY, ANY, HBM, HBM, HBM, HBM],
        3 << 32,
        5 << 20,
    )
    edge = (NY * CI, NX)
    back = call(
        back_kernel,
        (pltpu.HBM(edge, F32), pltpu.HBM(edge, F32), pltpu.HBM(edge, BF), pltpu.HBM(edge, BF)),
        [gbuf] * 2
        + [pltpu.VMEM((576, 256), BF)]
        + [pltpu.VMEM(edge, F32)] * 2
        + [pltpu.VMEM(edge, BF)] * 2
        + [DMA((5,)), DMA((4,))],
        [HBM] * 3,
        3 << 32,
        8 << 20,
        (HBM,) * 4,
    )
    finish = call(
        finish_kernel,
        pltpu.HBM((CI, 2, NY, NX), BF),
        [pltpu.VMEM(edge, F32)] * 2
        + [pltpu.VMEM(edge, BF)] * 2
        + [pltpu.VMEM((CI, 2, NY, NX), BF), DMA((4,)), DMA((4,))],
        [HBM, HBM, ANY, ANY],
        1 << 28,
        4 << 20,
        HBM,
    )
    prep = call(
        prep_kernel,
        (pltpu.HBM((768, 512), BF), pltpu.HBM((576, 256), BF), sds((CHUNKS, FROWS, NX), BF)),
        [
            pltpu.VMEM((512, 768), F32),
            pltpu.VMEM((768, 512), BF),
            pltpu.VMEM((576, 256), BF),
            pltpu.VMEM((3, 3, 3, CI, CO), BF),
            pltpu.VMEM((2048, NX), F32),
            DMA((7,)),
        ],
        [HBM] * 2,
        1 << 22,
        3 << 20,
        (HBM, HBM, VM),
    )
    out = call(
        out_kernel,
        (sds((CHUNKS * FROWS, NX), F32), sds((9, 3, CI, CO), F32), sds((1, CO), F32)),
        [],
        [VM],
        1 << 22,
        3 << 20,
    )
    inner, outer = turn(far(volumes[0]))
    far_inner, far_outer = swap(inner, outer)
    wf, wb, fin = prep(far(kernel.transpose(0, 1, 2, 4, 3)), far(finished_grads.reshape(2048, NX)))
    fin = exchange(fin, PLANE)
    x = (far_inner, far_outer, far(inner), far(outer))
    act, g0, g1 = forward(*x, far(wf), bias, far(cotangent[0]))
    taps = weight(*x, far(g0), far(g1))
    taps = exchange(taps.reshape(CHUNKS, TROWS, NX), PLANE)
    own0, own1, inner, outer = back(far(g0), far(g1), far(wb))
    far_inner, far_outer = swap(inner, outer)
    joined = join_b(fin, taps)
    joined = exchange(joined, COLUMN)
    joined = join_c(joined)
    joined = exchange(joined, PLANE)
    grad_volumes = finish(far(own0), far(own1), far_inner, far_outer)
    summed, grad_taps, grad_bias = out(joined)
    grad_kernel = grad_taps.reshape(3, 3, 3, CI, CO).transpose(0, 1, 2, 4, 3)
    return act[None], grad_volumes[None], grad_kernel, grad_bias.reshape(CO), summed.reshape(-1)


def solution(mesh):
    fine = Mesh(mesh.devices.reshape(2, 4, 8, 2, 2), ("yl", "x", "z", "yh", "c"))
    dp = ("yl", "x")
    slab = P(dp, None, SPACE, None, None)
    return jax.shard_map(
        layer,
        mesh=fine,
        in_specs=(slab, P(), P(), slab, P(dp, SPACE, None)),
        out_specs=(slab, slab, P(), P(), P()),
        check_vma=False,
    )
```

```python
import math

import jax
import jax.numpy as jnp
from jax import lax
from jax.experimental import pallas as pl
from jax.experimental.pallas import tpu as pltpu
from jax.sharding import Mesh, PartitionSpec as P

BF = jnp.bfloat16
F32 = jnp.float32
CI, CO, NY, NX = 32, 64, 48, 128
PADY = NY + 2
PLANE = ("yl", "x", "yh", "c")
COLUMN = "z"
CHUNKS, COLS = 32, 8
FROWS, TROWS = 64, 16
SPACE = ("z", "yh", "c")


def call(body, outs, scratch, specs, flops, nbytes, out_specs=None):
    return pl.pallas_call(
        body,
        out_shape=outs,
        in_specs=specs,
        out_specs=out_specs or jax.tree.map(lambda _: VM, outs),
        scratch_shapes=scratch,
        compiler_params=pltpu.CompilerParams(vmem_limit_bytes=48 << 20),
        cost_estimate=pl.CostEstimate(flops=flops, transcendentals=0, bytes_accessed=nbytes),
    )


VM = pl.BlockSpec(memory_space=pltpu.VMEM)
HBM = pl.BlockSpec(memory_space=pltpu.HBM)
ANY = pl.BlockSpec(memory_space=pl.ANY)
DMA = pltpu.SemaphoreType.DMA


def row_of(y, block, blocks):
    return pl.multiple_of(((y // 8) * blocks + block) * 64 + (y % 8) * 8, 8)


def by_core(copy_pairs, sems):
    core = lax.axis_index("c")
    for n, pairs in enumerate(copy_pairs):
        for side, (src, dst) in enumerate(pairs):

            @pl.when(core == side)
            def _(src=src, dst=dst, n=n):
                pltpu.make_async_copy(src, dst, sems.at[n]).start()

    return [pltpu.make_async_copy(*pairs[0], sems.at[n]) for n, pairs in enumerate(copy_pairs)]


def turn_kernel(x_ref, inner_ref, outer_ref, x, s0, s1, b0, b1, in_sem, out_sem):
    parts = [
        [
            pltpu.make_async_copy(
                x_ref.at[pl.ds(16 * n, 16), z], x.at[pl.ds(16 * n, 16), z], in_sem.at[2 * z + n]
            )
            for n in range(2)
        ]
        for z in range(2)
    ]
    for part in parts[0] + parts[1]:
        part.start()
    for b in (b0, b1):
        b[0:CI, :] = jnp.zeros((CI, NX), BF)
        b[CI * (NY + 1) : CI * PADY, :] = jnp.zeros((CI, NX), BF)
    outs = []
    for z, (s, b) in enumerate(((s0, b0), (s1, b1))):
        for n in range(2):
            parts[z][n].wait()
            for c in range(16 * n, 16 * n + 16):
                v = x[c, z].astype(F32)
                for m in range(NY // 8):
                    s[pl.ds((m * 4 + c // 8) * 64 + c % 8, 8, stride=8), :] = v[8 * m : 8 * m + 8]
        for y in range(NY):
            v = [s[pl.ds(((y // 8) * 4 + m) * 64 + (y % 8) * 8, 8), :] for m in range(4)]
            b[CI * (y + 1) : CI * (y + 2), :] = jnp.concatenate(v, axis=0).astype(BF)
        first, second = (outer_ref, inner_ref) if z == 0 else (inner_ref, outer_ref)
        outs += by_core([((b, first), (b, second))], out_sem.at[pl.ds(z, 1)])
    for out in outs:
        out.wait()


def shifted_sum(before, middle, after):
    lane = lax.broadcasted_iota(jnp.int32, middle.shape, 1)
    left = jnp.where(lane == 0, 0.0, pltpu.roll(before, 1, 1))
    right = jnp.where(lane == NX - 1, 0.0, pltpu.roll(after, NX - 1, 1))
    return middle + left + right


HALF = NY // 2 + 2


def halves(sources, buffers, width, sems):
    waits = []
    for half, rows in enumerate((pl.ds(0, HALF * width), pl.ds(HALF * width, (PADY - HALF) * width))):
        pairs = [
            tuple((src.at[rows], b.at[rows]) for src in both) for both, b in zip(sources, buffers)
        ]
        waits.append(by_core(pairs, sems.at[pl.ds(half * len(buffers), len(buffers))]))
    return waits


def x_sources(far_inner, far_outer, inner, outer):
    return ((far_outer, far_inner), (outer, inner), (inner, outer), (far_inner, far_outer))


def g_sources(inner, outer):
    return ((outer, inner), (inner, outer))


def forward_kernel(*refs):
    p_refs, (a_ref, bias_ref, cot_ref, act_ref, inner_ref, outer_ref) = refs[:4], refs[4:10]
    planes, (a, cot, act, g0, g1, s0, s1, in_sem, act_sem) = refs[10:14], refs[14:]
    a_copy = pltpu.make_async_copy(a_ref, a, in_sem.at[8])
    a_copy.start()
    first, second = halves(x_sources(*p_refs), planes, CI, in_sem)
    cot_copy = pltpu.make_async_copy(cot_ref, cot, in_sem.at[9])
    cot_copy.start()
    for g in (g0, g1):
        g[0:CO, :] = jnp.zeros((CO, NX), BF)
        g[CO * (NY + 1) : CO * PADY, :] = jnp.zeros((CO, NX), BF)

    def conv(q, _):
        sides = []
        for h in range(2):
            start = pl.multiple_of((2 * q + h) * (2 * CI), 2 * CI)
            sides.append(jnp.concatenate([p[pl.ds(start, 4 * CI), :] for p in planes], axis=0))
        rhs = jnp.concatenate(sides, axis=1)
        r = jnp.dot(a[...], rhs, preferred_element_type=F32)
        for h in range(2):
            rr = r[:, NX * h : NX * (h + 1)]
            y = shifted_sum(rr[0:256], rr[256:512], rr[512:768])
            for z, s in enumerate((s0, s1)):
                for p in range(2):
                    for m in range(8):
                        at = row_of(4 * q + 2 * h + p, m, 8)
                        s[pl.ds(at, 8), :] = y[128 * z + 64 * p + 8 * m : 128 * z + 64 * p + 8 * m + 8]
        return 0

    a_copy.wait()
    for part, lo in ((first, 0), (second, 6)):
        for copy in part:
            copy.wait()
        lax.fori_loop(lo, lo + 6, conv, 0, unroll=2)
    cot_copy.wait()

    def point(m, _):
        for n in range(8):
            o = m * 8 + n
            b = bias_ref[o]
            for z, s in ((0, s0), (1, s1)):
                for y in range(0, NY // 8, 2):
                    rows = [pl.ds(((y + u) * 8 + m) * 64 + n, 8, stride=8) for u in range(2)]
                    v = jnp.concatenate([s[r, :] for r in rows], axis=0) + b
                    t = jnp.tanh(0.5 * v)
                    soft = 0.7 * jnp.log(0.5 + 0.5 * jnp.abs(t))
                    act[o, z, 8 * y : 8 * y + 16, :] = (jnp.maximum(v, 0.3 * v) - soft).astype(BF)
                    grad = cot[o, z, 8 * y : 8 * y + 16, :].astype(F32) * (0.65 + 0.35 * t)
                    s[rows[0], :] = grad[0:8]
                    s[rows[1], :] = grad[8:16]
        some = pl.ds(8 * m, 8)
        pltpu.make_async_copy(act.at[some], act_ref.at[some], act_sem.at[m]).start()
        return 0

    lax.fori_loop(0, 8, point, 0)
    outs = []
    for n in range(8):
        some = pl.ds(8 * n, 8)
        outs.append(pltpu.make_async_copy(act.at[some], act_ref.at[some], act_sem.at[n]))
    for n, (g, s) in enumerate(((g0, s0), (g1, s1))):

        def rows_of(t, _, g=g, s=s):
            for y in range(8):
                v = [s[pl.ds((t * 8 + m) * 64 + y * 8, 8), :] for m in range(8)]
                at = pl.multiple_of((t * 8 + y + 1) * CO, CO)
                g[pl.ds(at, CO), :] = jnp.concatenate(v, axis=0).astype(BF)
            return 0

        lax.fori_loop(0, NY // 8, rows_of, 0)
        first, second = (outer_ref, inner_ref) if n == 0 else (inner_ref, outer_ref)
        outs += by_core([((g, first), (g, second))], act_sem.at[pl.ds(8 + n, 1)])
    for out in outs:
        out.wait()


def weight_kernel(*refs):
    p_refs, g_refs, out_ref = refs[:4], refs[4:6], refs[6]
    planes, gs_buf, acc, sems = refs[7:11], refs[11:13], refs[13], refs[14]
    first, second = halves(x_sources(*p_refs), planes, CI, sems)
    g_first, g_second = halves(g_sources(*g_refs), gs_buf, CO, sems.at[pl.ds(8, 4)])
    acc[...] = jnp.zeros_like(acc)
    lane = lax.broadcasted_iota(jnp.int32, (CO, NX), 1)

    def rows(q, _):
        gs, xs = [], []
        for y in range(4):
            ystart = pl.multiple_of((4 * q + y) * CI, CI)
            gstart = pl.multiple_of((4 * q + y + 1) * CO, CO)
            for z, g in enumerate(gs_buf):
                mid = g[pl.ds(gstart, CO), :]
                wide = mid.astype(F32)
                before = jnp.where(lane == NX - 1, 0.0, pltpu.roll(wide, NX - 1, 1)).astype(BF)
                after = jnp.where(lane == 0, 0.0, pltpu.roll(wide, 1, 1)).astype(BF)
                gs.append(jnp.concatenate([before, mid, after], axis=0))
                xs.append(
                    jnp.concatenate(
                        [planes[z + i][pl.ds(ystart, 3 * CI), :] for i in range(3)]
                        + [jnp.ones((16, NX), BF)],
                        axis=0,
                    )
                )
        acc[...] += lax.dot_general(
            jnp.concatenate(xs, axis=1),
            jnp.concatenate(gs, axis=1),
            (((1,), (1,)), ((), ())),
            preferred_element_type=F32,
        )
        return 0

    for part, lo in ((first + g_first, 0), (second + g_second, 24)):
        for copy in part:
            copy.wait()
        lax.fori_loop(lo // 4, lo // 4 + 6, rows, 0)
    out_ref[0:288, :] = acc[0:288, 0:128].astype(BF)
    side = acc[0:288, 128:192]
    tail = jnp.concatenate([side[160:288], jnp.zeros((32, CO), F32)], axis=0)
    out_ref[288:448, :] = jnp.concatenate([side[0:160], tail], axis=1).astype(BF)
    out_ref[448:464, :] = acc[288:304, 0:128].astype(BF)
    out_ref[464:512, :] = jnp.zeros((48, NX), BF)


def add_rows(s, q, z_rows, fresh):
    for h in range(2):
        rr = z_rows[:, NX * h : NX * (h + 1)]
        y = shifted_sum(rr[128:192], rr[64:128], rr[0:64])
        for p in range(2):
            for m in range(4):
                at = pl.ds(row_of(4 * q + 2 * h + p, m, 4), 8)
                part = y[32 * p + 8 * m : 32 * p + 8 * m + 8]
                s[at, :] = part if fresh else s[at, :] + part


def window(g, q):
    sides = [g[pl.ds(pl.multiple_of((2 * q + h) * (2 * CO), 2 * CO), 4 * CO), :] for h in range(2)]
    return jnp.concatenate(sides, axis=1)


def back_kernel(inner_ref, outer_ref, d_ref, own0_ref, own1_ref, g0, g1, d, s0, s1, sems, out_sem):
    d_copy = pltpu.make_async_copy(d_ref, d, sems.at[4])
    d_copy.start()
    first, second = halves(g_sources(inner_ref, outer_ref), (g0, g1), CO, sems)

    def conv(q, _):
        r = jnp.dot(d[192:576, :], window(g0, q), preferred_element_type=F32)
        r += jnp.dot(d[0:384, :], window(g1, q), preferred_element_type=F32)
        add_rows(s0, q, r[0:192], True)
        add_rows(s1, q, r[192:384], True)
        return 0

    d_copy.wait()
    for part, lo in ((first, 0), (second, 6)):
        for copy in part:
            copy.wait()
        lax.fori_loop(lo, lo + 6, conv, 0, unroll=2)
    outs = []
    for n, (s, own) in enumerate(((s0, own0_ref), (s1, own1_ref))):
        outs.append(pltpu.make_async_copy(s, own, out_sem.at[n]))
        outs[-1].start()
    for out in outs:
        out.wait()


def finish_kernel(own0_ref, own1_ref, inner_ref, outer_ref, d_ref, out_ref, *rest):
    s0, s1, low, high, d, buf, sems, out_sem = rest
    first, second = halves(g_sources(inner_ref, outer_ref), (low, high), CO, sems)
    first.append(pltpu.make_async_copy(d_ref, d, sems.at[4]))
    first[-1].start()
    for n, (own, s) in enumerate(((own0_ref, s0), (own1_ref, s1))):
        first.append(pltpu.make_async_copy(own, s, sems.at[5 + n]))
        first[-1].start()

    def conv(q, _):
        r0 = jnp.dot(d[384:576, :], window(low, q), preferred_element_type=F32)
        r1 = jnp.dot(d[0:192, :], window(high, q), preferred_element_type=F32)
        add_rows(s0, q, r0, False)
        add_rows(s1, q, r1, False)
        return 0

    for part, lo in ((first, 0), (second, 6)):
        for copy in part:
            copy.wait()
        lax.fori_loop(lo, lo + 6, conv, 0, unroll=2)

    def gather(m, _):
        for n in range(8):
            for z, s in ((0, s0), (1, s1)):
                v = [s[pl.ds((t * 4 + m) * 64 + n, 8, stride=8), :] for t in range(NY // 8)]
                buf[m * 8 + n, z] = jnp.concatenate(v, axis=0).astype(BF)
        some = pl.ds(8 * m, 8)
        pltpu.make_async_copy(buf.at[some], out_ref.at[some], out_sem.at[m]).start()
        return 0

    lax.fori_loop(0, 4, gather, 0)
    for n in range(4):
        some = pl.ds(8 * n, 8)
        pltpu.make_async_copy(buf.at[some], out_ref.at[some], out_sem.at[n]).wait()


def prep_kernel(w_hbm, f_hbm, a_out, d_out, out_ref, turned, a_ref, d_ref, w_ref, f_ref, sem):
    w_copy = pltpu.make_async_copy(w_hbm, w_ref, sem.at[2])
    w_copy.start()
    f_copies = [
        pltpu.make_async_copy(f_hbm.at[pl.ds(512 * n, 512)], f_ref.at[pl.ds(512 * n, 512)], sem.at[3 + n])
        for n in range(4)
    ]
    for copy in f_copies:
        copy.start()
    w_copy.wait()
    for z, hole in ((0, 3), (1, 0)):
        for k in range(3):
            col = (k * 2 + z) * 128
            turned[hole * 128 : hole * 128 + 128, col : col + 128] = jnp.zeros((128, 128), F32)
    for i in range(3):
        for k in range(3):
            w = [w_ref[i, j, k].astype(F32) for j in range(3)]
            none = jnp.zeros((CI, CO), F32)
            for s in range(4):
                pair = jnp.concatenate([w[s] if s < 3 else none, w[s - 1] if s else none], axis=1)
                y, p = ((0, 1), (1, 1), (0, 0), (1, 0))[s]
                row, col = i * 192 + (k * 2 + y) * CI, p * 128
                d_ref[row : row + CI, col : col + 128] = pair.astype(BF)
                for z in range(2):
                    row, col = ((i + z) * 4 + s) * CI, (k * 2 + z) * 128
                    turned[row : row + CI, col : col + 128] = pair
    d_copy = pltpu.make_async_copy(d_ref, d_out, sem.at[0])
    d_copy.start()
    a_ref[...] = turned[...].T.astype(BF)
    a_copy = pltpu.make_async_copy(a_ref, a_out, sem.at[1])
    a_copy.start()
    for n, copy in enumerate(f_copies):
        copy.wait()
        part = f_ref[512 * n : 512 * n + 512, :]
        out_ref[8 * n : 8 * n + 8] = part.reshape(8, FROWS, NX).astype(BF)
    d_copy.wait()
    a_copy.wait()


def join_b_kernel(f_ref, t_ref, out_ref):
    f = jnp.sum(f_ref[...].astype(F32), axis=0).astype(BF)
    t = jnp.sum(t_ref[...].astype(F32), axis=0).astype(BF)
    for n in range(COLS):
        out_ref[n, 0:FROWS] = f
        out_ref[n, FROWS:] = t


def join_c_kernel(in_ref, out_ref):
    both = jnp.sum(in_ref[...].astype(F32), axis=0).astype(BF)
    for n in range(CHUNKS):
        out_ref[n] = both


def out_kernel(in_ref, sum_ref, taps_ref, bias_ref):
    sum_ref[...] = in_ref[:, 0:FROWS, :].astype(F32).reshape(CHUNKS * FROWS, NX)
    scale = 1.0 / math.sqrt(8 * 64 * NY * NX)
    t = in_ref[:, FROWS:, :].astype(F32).reshape(CHUNKS * TROWS, NX) * scale
    for ij in range(9):
        two = t[ij * CI : ij * CI + CI]
        taps_ref[ij, 0] = two[:, 0:CO]
        taps_ref[ij, 1] = two[:, CO : 2 * CO]
        at, lane = (288 + ij * CI, 0) if ij < 5 else (288 + (ij - 5) * CI, CO)
        taps_ref[ij, 2] = t[at : at + CI, lane : lane + CO]
    bias_ref[...] = t[448:449, CO : 2 * CO]


def exchange(parts, axes):
    return lax.all_to_all(parts, axes, 0, 0)


def join_b(fin, taps):
    sds = jax.ShapeDtypeStruct((COLS, FROWS + TROWS, NX), BF)
    return call(join_b_kernel, sds, [], [VM] * 2, 1 << 20, 1 << 20)(fin, taps)


def join_c(parts):
    sds = jax.ShapeDtypeStruct((CHUNKS, FROWS + TROWS, NX), BF)
    return call(join_c_kernel, sds, [], [VM], 1 << 20, 1 << 20)(parts)


def swap(inner, outer):
    on_chip = [(i, i ^ 1) for i in range(32)]
    off_chip = [(i, i + 1) for i in range(1, 31, 2)] + [(i + 1, i) for i in range(1, 31, 2)]
    return lax.ppermute(inner, SPACE, on_chip), lax.ppermute(outer, SPACE, off_chip)


def far(x):
    return pltpu.with_memory_space_constraint(x, pltpu.HBM)


def layer(volumes, kernel, bias, cotangent, finished_grads):
    sds = jax.ShapeDtypeStruct
    x_plane = sds((PADY * CI, NX), BF)
    g_plane = sds((PADY * CO, NX), BF)
    turn = call(
        turn_kernel,
        (pltpu.HBM(x_plane.shape, BF), pltpu.HBM(x_plane.shape, BF)),
        [pltpu.VMEM((CI, 2, NY, NX), BF)]
        + [pltpu.VMEM((NY * CI, NX), F32)] * 2
        + [pltpu.VMEM((PADY * CI, NX), BF)] * 2
        + [DMA((4,)), DMA((2,))],
        [HBM],
        1 << 22,
        3 << 20,
        (HBM, HBM),
    )
    xbuf = pltpu.VMEM((PADY * CI, NX), BF)
    gbuf = pltpu.VMEM((PADY * CO, NX), BF)
    g_out = pltpu.HBM(g_plane.shape, BF)
    forward = call(
        forward_kernel,
        (pltpu.HBM((CO, 2, NY, NX), BF), g_out, g_out),
        [xbuf] * 4
        + [pltpu.VMEM((768, 512), BF)]
        + [pltpu.VMEM((CO, 2, NY, NX), BF)] * 2
        + [gbuf] * 2
        + [pltpu.VMEM((NY * CO, NX), F32)] * 2
        + [DMA((10,)), DMA((10,))],
        [ANY, ANY, HBM, HBM, HBM, pl.BlockSpec(memory_space=pltpu.SMEM), HBM],
        3 << 32,
        8 << 20,
        (HBM, HBM, HBM),
    )
    weight = call(
        weight_kernel,
        sds((512, NX), BF),
        [xbuf] * 4 + [gbuf] * 2 + [pltpu.VMEM((304, 192), F32), DMA((12,))],
        [ANY, ANY, HBM, HBM, HBM, HBM],
        3 << 32,
        5 << 20,
    )
    edge = (NY * CI, NX)
    dbuf = pltpu.VMEM((576, 256), BF)
    back = call(
        back_kernel,
        (pltpu.HBM(edge, F32), pltpu.HBM(edge, F32)),
        [gbuf] * 2 + [dbuf] + [pltpu.VMEM(edge, F32)] * 2 + [DMA((5,)), DMA((2,))],
        [HBM] * 3,
        2 << 32,
        6 << 20,
        (HBM,) * 2,
    )
    finish = call(
        finish_kernel,
        pltpu.HBM((CI, 2, NY, NX), BF),
        [pltpu.VMEM(edge, F32)] * 2
        + [gbuf] * 2
        + [dbuf, pltpu.VMEM((CI, 2, NY, NX), BF), DMA((7,)), DMA((4,))],
        [HBM, HBM, ANY, ANY, HBM],
        1 << 32,
        6 << 20,
        HBM,
    )
    prep = call(
        prep_kernel,
        (pltpu.HBM((768, 512), BF), pltpu.HBM((576, 256), BF), sds((CHUNKS, FROWS, NX), BF)),
        [
            pltpu.VMEM((512, 768), F32),
            pltpu.VMEM((768, 512), BF),
            pltpu.VMEM((576, 256), BF),
            pltpu.VMEM((3, 3, 3, CI, CO), BF),
            pltpu.VMEM((2048, NX), F32),
            DMA((7,)),
        ],
        [HBM] * 2,
        1 << 22,
        3 << 20,
        (HBM, HBM, VM),
    )
    out = call(
        out_kernel,
        (sds((CHUNKS * FROWS, NX), F32), sds((9, 3, CI, CO), F32), sds((1, CO), F32)),
        [],
        [VM],
        1 << 22,
        3 << 20,
    )
    inner, outer = turn(far(volumes[0]))
    far_inner, far_outer = swap(inner, outer)
    wf, wb, fin = prep(far(kernel.transpose(0, 1, 2, 4, 3)), far(finished_grads.reshape(2048, NX)))
    fin = exchange(fin, PLANE)
    x = (far_inner, far_outer, far(inner), far(outer))
    act, inner, outer = forward(*x, far(wf), bias, far(cotangent[0]))
    far_inner, far_outer = swap(inner, outer)
    taps = weight(*x, far(inner), far(outer))
    taps = exchange(taps.reshape(CHUNKS, TROWS, NX), PLANE)
    own0, own1 = back(far(inner), far(outer), far(wb))
    joined = join_b(fin, taps)
    joined = exchange(joined, COLUMN)
    joined = join_c(joined)
    joined = exchange(joined, PLANE)
    grad_volumes = finish(far(own0), far(own1), far_inner, far_outer, far(wb))
    summed, grad_taps, grad_bias = out(joined)
    grad_kernel = grad_taps.reshape(3, 3, 3, CI, CO).transpose(0, 1, 2, 4, 3)
    return act[None], grad_volumes[None], grad_kernel, grad_bias.reshape(CO), summed.reshape(-1)


def solution(mesh):
    fine = Mesh(mesh.devices.reshape(2, 4, 8, 2, 2), ("yl", "x", "z", "yh", "c"))
    dp = ("yl", "x")
    slab = P(dp, None, SPACE, None, None)
    return jax.shard_map(
        layer,
        mesh=fine,
        in_specs=(slab, P(), P(), slab, P(dp, SPACE, None)),
        out_specs=(slab, slab, P(), P(), P()),
        check_vma=False,
    )
```

```python
import math

import jax
import jax.numpy as jnp
from jax import lax
from jax.experimental import pallas as pl
from jax.experimental.pallas import tpu as pltpu
from jax.sharding import Mesh, PartitionSpec as P

BF = jnp.bfloat16
F32 = jnp.float32
CI, CO, NY, NX = 32, 64, 48, 128
PADY = NY + 2
PLANE = ("yl", "x", "zl", "yh", "c")
COLUMN = "zh"
CHUNKS, COLS = 64, 4
FROWS, TROWS = 2048 // CHUNKS, 512 // CHUNKS
SPACE = ("zh", "zl", "yh", "c")


def call(body, outs, scratch, specs, flops, nbytes, out_specs=None):
    return pl.pallas_call(
        body,
        out_shape=outs,
        in_specs=specs,
        out_specs=out_specs or jax.tree.map(lambda _: VM, outs),
        scratch_shapes=scratch,
        compiler_params=pltpu.CompilerParams(vmem_limit_bytes=48 << 20),
        cost_estimate=pl.CostEstimate(flops=flops, transcendentals=0, bytes_accessed=nbytes),
    )


VM = pl.BlockSpec(memory_space=pltpu.VMEM)
HBM = pl.BlockSpec(memory_space=pltpu.HBM)
ANY = pl.BlockSpec(memory_space=pl.ANY)
DMA = pltpu.SemaphoreType.DMA


def row_of(y, block, blocks):
    return pl.multiple_of(((y // 8) * blocks + block) * 64 + (y % 8) * 8, 8)


def by_core(copy_pairs, sems):
    core = lax.axis_index("c")
    for n, pairs in enumerate(copy_pairs):
        for side, (src, dst) in enumerate(pairs):

            @pl.when(core == side)
            def _(src=src, dst=dst, n=n):
                pltpu.make_async_copy(src, dst, sems.at[n]).start()

    return [pltpu.make_async_copy(*pairs[0], sems.at[n]) for n, pairs in enumerate(copy_pairs)]


def turn_kernel(x_ref, inner_ref, outer_ref, x, s0, s1, b0, b1, in_sem, out_sem):
    parts = [
        [
            pltpu.make_async_copy(
                x_ref.at[pl.ds(16 * n, 16), z], x.at[pl.ds(16 * n, 16), z], in_sem.at[2 * z + n]
            )
            for n in range(2)
        ]
        for z in range(2)
    ]
    for part in parts[0] + parts[1]:
        part.start()
    for b in (b0, b1):
        b[0:CI, :] = jnp.zeros((CI, NX), BF)
        b[CI * (NY + 1) : CI * PADY, :] = jnp.zeros((CI, NX), BF)
    outs = []
    for z, (s, b) in enumerate(((s0, b0), (s1, b1))):
        for n in range(2):
            parts[z][n].wait()
            for c in range(16 * n, 16 * n + 16):
                v = x[c, z].astype(F32)
                for m in range(NY // 8):
                    s[pl.ds((m * 4 + c // 8) * 64 + c % 8, 8, stride=8), :] = v[8 * m : 8 * m + 8]
        for y in range(NY):
            v = [s[pl.ds(((y // 8) * 4 + m) * 64 + (y % 8) * 8, 8), :] for m in range(4)]
            b[CI * (y + 1) : CI * (y + 2), :] = jnp.concatenate(v, axis=0).astype(BF)
        first, second = (outer_ref, inner_ref) if z == 0 else (inner_ref, outer_ref)
        outs += by_core([((b, first), (b, second))], out_sem.at[pl.ds(z, 1)])
    for out in outs:
        out.wait()


def shifted_sum(before, middle, after):
    lane = lax.broadcasted_iota(jnp.int32, middle.shape, 1)
    left = jnp.where(lane == 0, 0.0, pltpu.roll(before, 1, 1))
    right = jnp.where(lane == NX - 1, 0.0, pltpu.roll(after, NX - 1, 1))
    return middle + left + right


HALF = NY // 2 + 2


def halves(sources, buffers, width, sems):
    waits = []
    for half, rows in enumerate((pl.ds(0, HALF * width), pl.ds(HALF * width, (PADY - HALF) * width))):
        pairs = [
            tuple((src.at[rows], b.at[rows]) for src in both) for both, b in zip(sources, buffers)
        ]
        waits.append(by_core(pairs, sems.at[pl.ds(half * len(buffers), len(buffers))]))
    return waits


def x_sources(far_inner, far_outer, inner, outer):
    return ((far_outer, far_inner), (outer, inner), (inner, outer), (far_inner, far_outer))


def g_sources(inner, outer):
    return ((outer, inner), (inner, outer))


def forward_kernel(*refs):
    p_refs, (a_ref, bias_ref, cot_ref, act_ref, inner_ref, outer_ref) = refs[:4], refs[4:10]
    planes, (a, cot, act, g0, g1, s0, s1, in_sem, act_sem) = refs[10:14], refs[14:]
    a_copy = pltpu.make_async_copy(a_ref, a, in_sem.at[8])
    a_copy.start()
    first, second = halves(x_sources(*p_refs), planes, CI, in_sem)
    cot_copy = pltpu.make_async_copy(cot_ref, cot, in_sem.at[9])
    cot_copy.start()
    for g in (g0, g1):
        g[0:CO, :] = jnp.zeros((CO, NX), BF)
        g[CO * (NY + 1) : CO * PADY, :] = jnp.zeros((CO, NX), BF)

    def conv(q, _):
        sides = []
        for h in range(2):
            start = pl.multiple_of((2 * q + h) * (2 * CI), 2 * CI)
            sides.append(jnp.concatenate([p[pl.ds(start, 4 * CI), :] for p in planes], axis=0))
        rhs = jnp.concatenate(sides, axis=1)
        r = jnp.dot(a[...], rhs, preferred_element_type=F32)
        for h in range(2):
            rr = r[:, NX * h : NX * (h + 1)]
            y = shifted_sum(rr[0:256], rr[256:512], rr[512:768])
            for z, s in enumerate((s0, s1)):
                for p in range(2):
                    for m in range(8):
                        at = row_of(4 * q + 2 * h + p, m, 8)
                        s[pl.ds(at, 8), :] = y[128 * z + 64 * p + 8 * m : 128 * z + 64 * p + 8 * m + 8]
        return 0

    a_copy.wait()
    for part, lo in ((first, 0), (second, 6)):
        for copy in part:
            copy.wait()
        lax.fori_loop(lo, lo + 6, conv, 0, unroll=2)
    cot_copy.wait()

    def point(m, _):
        for n in range(8):
            o = m * 8 + n
            b = bias_ref[o]
            for z, s in ((0, s0), (1, s1)):
                for y in range(0, NY // 8, 2):
                    rows = [pl.ds(((y + u) * 8 + m) * 64 + n, 8, stride=8) for u in range(2)]
                    v = jnp.concatenate([s[r, :] for r in rows], axis=0) + b
                    t = jnp.tanh(0.5 * v)
                    soft = 0.7 * jnp.log(0.5 + 0.5 * jnp.abs(t))
                    act[o, z, 8 * y : 8 * y + 16, :] = (jnp.maximum(v, 0.3 * v) - soft).astype(BF)
                    grad = cot[o, z, 8 * y : 8 * y + 16, :].astype(F32) * (0.65 + 0.35 * t)
                    s[rows[0], :] = grad[0:8]
                    s[rows[1], :] = grad[8:16]
        some = pl.ds(8 * m, 8)
        pltpu.make_async_copy(act.at[some], act_ref.at[some], act_sem.at[m]).start()
        return 0

    lax.fori_loop(0, 8, point, 0)
    outs = []
    for n in range(8):
        some = pl.ds(8 * n, 8)
        outs.append(pltpu.make_async_copy(act.at[some], act_ref.at[some], act_sem.at[n]))
    for n, (g, s) in enumerate(((g0, s0), (g1, s1))):

        def rows_of(t, _, g=g, s=s):
            for y in range(8):
                v = [s[pl.ds((t * 8 + m) * 64 + y * 8, 8), :] for m in range(8)]
                at = pl.multiple_of((t * 8 + y + 1) * CO, CO)
                g[pl.ds(at, CO), :] = jnp.concatenate(v, axis=0).astype(BF)
            return 0

        lax.fori_loop(0, NY // 8, rows_of, 0)
        first, second = (outer_ref, inner_ref) if n == 0 else (inner_ref, outer_ref)
        outs += by_core([((g, first), (g, second))], act_sem.at[pl.ds(8 + n, 1)])
    for out in outs:
        out.wait()


def weight_kernel(*refs):
    p_refs, g_refs, out_ref = refs[:4], refs[4:6], refs[6]
    planes, gs_buf, acc, sems = refs[7:11], refs[11:13], refs[13], refs[14]
    first, second = halves(x_sources(*p_refs), planes, CI, sems)
    g_first, g_second = halves(g_sources(*g_refs), gs_buf, CO, sems.at[pl.ds(8, 4)])
    acc[...] = jnp.zeros_like(acc)
    lane = lax.broadcasted_iota(jnp.int32, (CO, NX), 1)

    def rows(q, _):
        gs, xs = [], []
        for y in range(4):
            ystart = pl.multiple_of((4 * q + y) * CI, CI)
            gstart = pl.multiple_of((4 * q + y + 1) * CO, CO)
            for z, g in enumerate(gs_buf):
                mid = g[pl.ds(gstart, CO), :]
                wide = mid.astype(F32)
                before = jnp.where(lane == NX - 1, 0.0, pltpu.roll(wide, NX - 1, 1)).astype(BF)
                after = jnp.where(lane == 0, 0.0, pltpu.roll(wide, 1, 1)).astype(BF)
                gs.append(jnp.concatenate([before, mid, after], axis=0))
                xs.append(
                    jnp.concatenate(
                        [planes[z + i][pl.ds(ystart, 3 * CI), :] for i in range(3)]
                        + [jnp.ones((16, NX), BF)],
                        axis=0,
                    )
                )
        acc[...] += lax.dot_general(
            jnp.concatenate(xs, axis=1),
            jnp.concatenate(gs, axis=1),
            (((1,), (1,)), ((), ())),
            preferred_element_type=F32,
        )
        return 0

    for part, lo in ((first + g_first, 0), (second + g_second, 24)):
        for copy in part:
            copy.wait()
        lax.fori_loop(lo // 4, lo // 4 + 6, rows, 0)
    out_ref[0:288, :] = acc[0:288, 0:128].astype(BF)
    side = acc[0:288, 128:192]
    tail = jnp.concatenate([side[160:288], jnp.zeros((32, CO), F32)], axis=0)
    out_ref[288:448, :] = jnp.concatenate([side[0:160], tail], axis=1).astype(BF)
    out_ref[448:464, :] = acc[288:304, 0:128].astype(BF)
    out_ref[464:512, :] = jnp.zeros((48, NX), BF)


def add_rows(s, q, z_rows, fresh):
    for h in range(2):
        rr = z_rows[:, NX * h : NX * (h + 1)]
        y = shifted_sum(rr[128:192], rr[64:128], rr[0:64])
        for p in range(2):
            for m in range(4):
                at = pl.ds(row_of(4 * q + 2 * h + p, m, 4), 8)
                part = y[32 * p + 8 * m : 32 * p + 8 * m + 8]
                s[at, :] = part if fresh else s[at, :] + part


def window(g, q):
    sides = [g[pl.ds(pl.multiple_of((2 * q + h) * (2 * CO), 2 * CO), 4 * CO), :] for h in range(2)]
    return jnp.concatenate(sides, axis=1)


def back_kernel(inner_ref, outer_ref, d_ref, own0_ref, own1_ref, g0, g1, d, s0, s1, sems, out_sem):
    d_copy = pltpu.make_async_copy(d_ref, d, sems.at[4])
    d_copy.start()
    first, second = halves(g_sources(inner_ref, outer_ref), (g0, g1), CO, sems)

    def conv(q, _):
        r = jnp.dot(d[192:576, :], window(g0, q), preferred_element_type=F32)
        r += jnp.dot(d[0:384, :], window(g1, q), preferred_element_type=F32)
        add_rows(s0, q, r[0:192], True)
        add_rows(s1, q, r[192:384], True)
        return 0

    d_copy.wait()
    for part, lo in ((first, 0), (second, 6)):
        for copy in part:
            copy.wait()
        lax.fori_loop(lo, lo + 6, conv, 0, unroll=2)
    outs = []
    for n, (s, own) in enumerate(((s0, own0_ref), (s1, own1_ref))):
        outs.append(pltpu.make_async_copy(s, own, out_sem.at[n]))
        outs[-1].start()
    for out in outs:
        out.wait()


def finish_kernel(own0_ref, own1_ref, inner_ref, outer_ref, d_ref, out_ref, *rest):
    s0, s1, low, high, d, buf, sems, out_sem = rest
    first, second = halves(g_sources(inner_ref, outer_ref), (low, high), CO, sems)
    first.append(pltpu.make_async_copy(d_ref, d, sems.at[4]))
    first[-1].start()
    for n, (own, s) in enumerate(((own0_ref, s0), (own1_ref, s1))):
        first.append(pltpu.make_async_copy(own, s, sems.at[5 + n]))
        first[-1].start()

    def conv(q, _):
        r0 = jnp.dot(d[384:576, :], window(low, q), preferred_element_type=F32)
        r1 = jnp.dot(d[0:192, :], window(high, q), preferred_element_type=F32)
        add_rows(s0, q, r0, False)
        add_rows(s1, q, r1, False)
        return 0

    for part, lo in ((first, 0), (second, 6)):
        for copy in part:
            copy.wait()
        lax.fori_loop(lo, lo + 6, conv, 0, unroll=2)

    def gather(m, _):
        for n in range(8):
            for z, s in ((0, s0), (1, s1)):
                v = [s[pl.ds((t * 4 + m) * 64 + n, 8, stride=8), :] for t in range(NY // 8)]
                buf[m * 8 + n, z] = jnp.concatenate(v, axis=0).astype(BF)
        some = pl.ds(8 * m, 8)
        pltpu.make_async_copy(buf.at[some], out_ref.at[some], out_sem.at[m]).start()
        return 0

    lax.fori_loop(0, 4, gather, 0)
    for n in range(4):
        some = pl.ds(8 * n, 8)
        pltpu.make_async_copy(buf.at[some], out_ref.at[some], out_sem.at[n]).wait()


def prep_kernel(w_hbm, f_hbm, a_out, d_out, out_ref, turned, a_ref, d_ref, w_ref, f_ref, sem):
    w_copy = pltpu.make_async_copy(w_hbm, w_ref, sem.at[2])
    w_copy.start()
    f_copies = [
        pltpu.make_async_copy(f_hbm.at[pl.ds(512 * n, 512)], f_ref.at[pl.ds(512 * n, 512)], sem.at[3 + n])
        for n in range(4)
    ]
    for copy in f_copies:
        copy.start()
    w_copy.wait()
    for z, hole in ((0, 3), (1, 0)):
        for k in range(3):
            col = (k * 2 + z) * 128
            turned[hole * 128 : hole * 128 + 128, col : col + 128] = jnp.zeros((128, 128), F32)
    for i in range(3):
        for k in range(3):
            w = [w_ref[i, j, k].astype(F32) for j in range(3)]
            none = jnp.zeros((CI, CO), F32)
            for s in range(4):
                pair = jnp.concatenate([w[s] if s < 3 else none, w[s - 1] if s else none], axis=1)
                y, p = ((0, 1), (1, 1), (0, 0), (1, 0))[s]
                row, col = i * 192 + (k * 2 + y) * CI, p * 128
                d_ref[row : row + CI, col : col + 128] = pair.astype(BF)
                for z in range(2):
                    row, col = ((i + z) * 4 + s) * CI, (k * 2 + z) * 128
                    turned[row : row + CI, col : col + 128] = pair
    d_copy = pltpu.make_async_copy(d_ref, d_out, sem.at[0])
    d_copy.start()
    a_ref[...] = turned[...].T.astype(BF)
    a_copy = pltpu.make_async_copy(a_ref, a_out, sem.at[1])
    a_copy.start()
    for n, copy in enumerate(f_copies):
        copy.wait()
        part = f_ref[512 * n : 512 * n + 512, :]
        some = CHUNKS // 4
        out_ref[some * n : some * n + some] = part.reshape(some, FROWS, NX).astype(BF)
    d_copy.wait()
    a_copy.wait()


def join_b_kernel(f_ref, t_ref, out_ref):
    f = jnp.sum(f_ref[...].astype(F32), axis=0).astype(BF)
    t = jnp.sum(t_ref[...].astype(F32), axis=0).astype(BF)
    for n in range(COLS):
        out_ref[n, 0:FROWS] = f
        out_ref[n, FROWS:] = t


def join_c_kernel(in_ref, out_ref):
    both = jnp.sum(in_ref[...].astype(F32), axis=0).astype(BF)
    for n in range(CHUNKS):
        out_ref[n] = both


def out_kernel(in_ref, sum_ref, taps_ref, bias_ref):
    sum_ref[...] = in_ref[:, 0:FROWS, :].astype(F32).reshape(CHUNKS * FROWS, NX)
    scale = 1.0 / math.sqrt(8 * 64 * NY * NX)
    t = in_ref[:, FROWS:, :].astype(F32).reshape(CHUNKS * TROWS, NX) * scale
    for ij in range(9):
        two = t[ij * CI : ij * CI + CI]
        taps_ref[ij, 0] = two[:, 0:CO]
        taps_ref[ij, 1] = two[:, CO : 2 * CO]
        at, lane = (288 + ij * CI, 0) if ij < 5 else (288 + (ij - 5) * CI, CO)
        taps_ref[ij, 2] = t[at : at + CI, lane : lane + CO]
    bias_ref[...] = t[448:449, CO : 2 * CO]


def exchange(parts, axes):
    return lax.all_to_all(parts, axes, 0, 0)


def join_b(fin, taps):
    sds = jax.ShapeDtypeStruct((COLS, FROWS + TROWS, NX), BF)
    return call(join_b_kernel, sds, [], [VM] * 2, 1 << 20, 1 << 20)(fin, taps)


def join_c(parts):
    sds = jax.ShapeDtypeStruct((CHUNKS, FROWS + TROWS, NX), BF)
    return call(join_c_kernel, sds, [], [VM], 1 << 20, 1 << 20)(parts)


def swap(inner, outer):
    on_chip = [(i, i ^ 1) for i in range(32)]
    off_chip = [(i, i + 1) for i in range(1, 31, 2)] + [(i + 1, i) for i in range(1, 31, 2)]
    return lax.ppermute(inner, SPACE, on_chip), lax.ppermute(outer, SPACE, off_chip)


def far(x):
    return pltpu.with_memory_space_constraint(x, pltpu.HBM)


def layer(volumes, kernel, bias, cotangent, finished_grads):
    sds = jax.ShapeDtypeStruct
    x_plane = sds((PADY * CI, NX), BF)
    g_plane = sds((PADY * CO, NX), BF)
    turn = call(
        turn_kernel,
        (pltpu.HBM(x_plane.shape, BF), pltpu.HBM(x_plane.shape, BF)),
        [pltpu.VMEM((CI, 2, NY, NX), BF)]
        + [pltpu.VMEM((NY * CI, NX), F32)] * 2
        + [pltpu.VMEM((PADY * CI, NX), BF)] * 2
        + [DMA((4,)), DMA((2,))],
        [HBM],
        1 << 22,
        3 << 20,
        (HBM, HBM),
    )
    xbuf = pltpu.VMEM((PADY * CI, NX), BF)
    gbuf = pltpu.VMEM((PADY * CO, NX), BF)
    g_out = pltpu.HBM(g_plane.shape, BF)
    forward = call(
        forward_kernel,
        (pltpu.HBM((CO, 2, NY, NX), BF), g_out, g_out),
        [xbuf] * 4
        + [pltpu.VMEM((768, 512), BF)]
        + [pltpu.VMEM((CO, 2, NY, NX), BF)] * 2
        + [gbuf] * 2
        + [pltpu.VMEM((NY * CO, NX), F32)] * 2
        + [DMA((10,)), DMA((10,))],
        [ANY, ANY, HBM, HBM, HBM, pl.BlockSpec(memory_space=pltpu.SMEM), HBM],
        3 << 32,
        8 << 20,
        (HBM, HBM, HBM),
    )
    weight = call(
        weight_kernel,
        sds((512, NX), BF),
        [xbuf] * 4 + [gbuf] * 2 + [pltpu.VMEM((304, 192), F32), DMA((12,))],
        [ANY, ANY, HBM, HBM, HBM, HBM],
        3 << 32,
        5 << 20,
    )
    edge = (NY * CI, NX)
    dbuf = pltpu.VMEM((576, 256), BF)
    back = call(
        back_kernel,
        (pltpu.HBM(edge, F32), pltpu.HBM(edge, F32)),
        [gbuf] * 2 + [dbuf] + [pltpu.VMEM(edge, F32)] * 2 + [DMA((5,)), DMA((2,))],
        [HBM] * 3,
        2 << 32,
        6 << 20,
        (HBM,) * 2,
    )
    finish = call(
        finish_kernel,
        pltpu.HBM((CI, 2, NY, NX), BF),
        [pltpu.VMEM(edge, F32)] * 2
        + [gbuf] * 2
        + [dbuf, pltpu.VMEM((CI, 2, NY, NX), BF), DMA((7,)), DMA((4,))],
        [HBM, HBM, ANY, ANY, HBM],
        1 << 32,
        6 << 20,
        HBM,
    )
    prep = call(
        prep_kernel,
        (pltpu.HBM((768, 512), BF), pltpu.HBM((576, 256), BF), sds((CHUNKS, FROWS, NX), BF)),
        [
            pltpu.VMEM((512, 768), F32),
            pltpu.VMEM((768, 512), BF),
            pltpu.VMEM((576, 256), BF),
            pltpu.VMEM((3, 3, 3, CI, CO), BF),
            pltpu.VMEM((2048, NX), F32),
            DMA((7,)),
        ],
        [HBM] * 2,
        1 << 22,
        3 << 20,
        (HBM, HBM, VM),
    )
    out = call(
        out_kernel,
        (sds((CHUNKS * FROWS, NX), F32), sds((9, 3, CI, CO), F32), sds((1, CO), F32)),
        [],
        [VM],
        1 << 22,
        3 << 20,
    )
    inner, outer = turn(far(volumes[0]))
    far_inner, far_outer = swap(inner, outer)
    wf, wb, fin = prep(far(kernel.transpose(0, 1, 2, 4, 3)), far(finished_grads.reshape(2048, NX)))
    fin = exchange(fin, PLANE)
    x = (far_inner, far_outer, far(inner), far(outer))
    act, inner, outer = forward(*x, far(wf), bias, far(cotangent[0]))
    far_inner, far_outer = swap(inner, outer)
    taps = weight(*x, far(inner), far(outer))
    taps = exchange(taps.reshape(CHUNKS, TROWS, NX), PLANE)
    own0, own1 = back(far(inner), far(outer), far(wb))
    joined = join_b(fin, taps)
    joined = exchange(joined, COLUMN)
    joined = join_c(joined)
    joined = exchange(joined, PLANE)
    grad_volumes = finish(far(own0), far(own1), far_inner, far_outer, far(wb))
    summed, grad_taps, grad_bias = out(joined)
    grad_kernel = grad_taps.reshape(3, 3, 3, CI, CO).transpose(0, 1, 2, 4, 3)
    return act[None], grad_volumes[None], grad_kernel, grad_bias.reshape(CO), summed.reshape(-1)


def solution(mesh):
    fine = Mesh(mesh.devices.reshape(2, 4, 4, 2, 2, 2), ("yl", "x") + SPACE)
    dp = ("yl", "x")
    slab = P(dp, None, SPACE, None, None)
    return jax.shard_map(
        layer,
        mesh=fine,
        in_specs=(slab, P(), P(), slab, P(dp, SPACE, None)),
        out_specs=(slab, slab, P(), P(), P()),
        check_vma=False,
    )
```

```python
import math

import jax
import jax.numpy as jnp
from jax import lax
from jax.experimental import pallas as pl
from jax.experimental.pallas import tpu as pltpu
from jax.sharding import Mesh, PartitionSpec as P

BF = jnp.bfloat16
F32 = jnp.float32
CI, CO, NY, NX = 32, 64, 48, 128
PADY = NY + 2
PLANE = ("yl", "x", "zl", "yh", "c")
COLUMN = "zh"
CHUNKS, COLS = 64, 4
FROWS, TROWS = 2048 // CHUNKS, 512 // CHUNKS
SPACE = ("zh", "zl", "yh", "c")


def call(body, outs, scratch, specs, flops, nbytes, out_specs=None):
    return pl.pallas_call(
        body,
        out_shape=outs,
        in_specs=specs,
        out_specs=out_specs or jax.tree.map(lambda _: VM, outs),
        scratch_shapes=scratch,
        compiler_params=pltpu.CompilerParams(vmem_limit_bytes=48 << 20),
        cost_estimate=pl.CostEstimate(flops=flops, transcendentals=0, bytes_accessed=nbytes),
    )


VM = pl.BlockSpec(memory_space=pltpu.VMEM)
HBM = pl.BlockSpec(memory_space=pltpu.HBM)
ANY = pl.BlockSpec(memory_space=pl.ANY)
DMA = pltpu.SemaphoreType.DMA


def row_of(y, block, blocks):
    return pl.multiple_of(((y // 8) * blocks + block) * 64 + (y % 8) * 8, 8)


def by_core(copy_pairs, sems):
    core = lax.axis_index("c")
    for n, pairs in enumerate(copy_pairs):
        for side, (src, dst) in enumerate(pairs):

            @pl.when(core == side)
            def _(src=src, dst=dst, n=n):
                pltpu.make_async_copy(src, dst, sems.at[n]).start()

    return [pltpu.make_async_copy(*pairs[0], sems.at[n]) for n, pairs in enumerate(copy_pairs)]


def turn_kernel(x_ref, inner_ref, outer_ref, x, s0, s1, b0, b1, in_sem, out_sem):
    parts = [
        [
            pltpu.make_async_copy(
                x_ref.at[pl.ds(16 * n, 16), z], x.at[pl.ds(16 * n, 16), z], in_sem.at[2 * z + n]
            )
            for n in range(2)
        ]
        for z in range(2)
    ]
    for part in parts[0] + parts[1]:
        part.start()
    for b in (b0, b1):
        b[0:CI, :] = jnp.zeros((CI, NX), BF)
        b[CI * (NY + 1) : CI * PADY, :] = jnp.zeros((CI, NX), BF)
    outs = []
    for z, (s, b) in enumerate(((s0, b0), (s1, b1))):
        for n in range(2):
            parts[z][n].wait()
            for c in range(16 * n, 16 * n + 16):
                v = x[c, z].astype(F32)
                for m in range(NY // 8):
                    s[pl.ds((m * 4 + c // 8) * 64 + c % 8, 8, stride=8), :] = v[8 * m : 8 * m + 8]
        for y in range(NY):
            v = [s[pl.ds(((y // 8) * 4 + m) * 64 + (y % 8) * 8, 8), :] for m in range(4)]
            b[CI * (y + 1) : CI * (y + 2), :] = jnp.concatenate(v, axis=0).astype(BF)
        first, second = (outer_ref, inner_ref) if z == 0 else (inner_ref, outer_ref)
        outs += by_core([((b, first), (b, second))], out_sem.at[pl.ds(z, 1)])
    for out in outs:
        out.wait()


def shifted_sum(before, middle, after):
    lane = lax.broadcasted_iota(jnp.int32, middle.shape, 1)
    left = jnp.where(lane == 0, 0.0, pltpu.roll(before, 1, 1))
    right = jnp.where(lane == NX - 1, 0.0, pltpu.roll(after, NX - 1, 1))
    return middle + left + right


HALF = NY // 2 + 2


def halves(sources, buffers, width, sems):
    waits = []
    for half, rows in enumerate((pl.ds(0, HALF * width), pl.ds(HALF * width, (PADY - HALF) * width))):
        pairs = [
            tuple((src.at[rows], b.at[rows]) for src in both) for both, b in zip(sources, buffers)
        ]
        waits.append(by_core(pairs, sems.at[pl.ds(half * len(buffers), len(buffers))]))
    return waits


def x_sources(far_inner, far_outer, inner, outer):
    return ((far_outer, far_inner), (outer, inner), (inner, outer), (far_inner, far_outer))


def g_sources(inner, outer):
    return ((outer, inner), (inner, outer))


def forward_kernel(*refs):
    p_refs, (a_ref, bias_ref, cot_ref, act_ref, inner_ref, outer_ref) = refs[:4], refs[4:10]
    planes, (a, cot, act, g0, g1, s0, s1, in_sem, act_sem) = refs[10:14], refs[14:]
    a_copy = pltpu.make_async_copy(a_ref, a, in_sem.at[8])
    a_copy.start()
    first, second = halves(x_sources(*p_refs), planes, CI, in_sem)
    cot_copy = pltpu.make_async_copy(cot_ref, cot, in_sem.at[9])
    cot_copy.start()
    for g in (g0, g1):
        g[0:CO, :] = jnp.zeros((CO, NX), BF)
        g[CO * (NY + 1) : CO * PADY, :] = jnp.zeros((CO, NX), BF)

    def conv(q, _):
        sides = []
        for h in range(2):
            start = pl.multiple_of((2 * q + h) * (2 * CI), 2 * CI)
            sides.append(jnp.concatenate([p[pl.ds(start, 4 * CI), :] for p in planes], axis=0))
        rhs = jnp.concatenate(sides, axis=1)
        r = jnp.dot(a[...], rhs, preferred_element_type=F32)
        for h in range(2):
            rr = r[:, NX * h : NX * (h + 1)]
            y = shifted_sum(rr[0:256], rr[256:512], rr[512:768])
            for z, s in enumerate((s0, s1)):
                for p in range(2):
                    for m in range(8):
                        at = row_of(4 * q + 2 * h + p, m, 8)
                        s[pl.ds(at, 8), :] = y[128 * z + 64 * p + 8 * m : 128 * z + 64 * p + 8 * m + 8]
        return 0

    a_copy.wait()
    for part, lo in ((first, 0), (second, 6)):
        for copy in part:
            copy.wait()
        lax.fori_loop(lo, lo + 6, conv, 0, unroll=3)
    cot_copy.wait()

    def point(m, _):
        for n in range(8):
            o = m * 8 + n
            b = bias_ref[o]
            for z, s in ((0, s0), (1, s1)):
                for y in range(0, NY // 8, 2):
                    rows = [pl.ds(((y + u) * 8 + m) * 64 + n, 8, stride=8) for u in range(2)]
                    v = jnp.concatenate([s[r, :] for r in rows], axis=0) + b
                    t = jnp.tanh(0.5 * v)
                    soft = 0.7 * jnp.log(0.5 + 0.5 * jnp.abs(t))
                    act[o, z, 8 * y : 8 * y + 16, :] = (jnp.maximum(v, 0.3 * v) - soft).astype(BF)
                    grad = cot[o, z, 8 * y : 8 * y + 16, :].astype(F32) * (0.65 + 0.35 * t)
                    s[rows[0], :] = grad[0:8]
                    s[rows[1], :] = grad[8:16]
        some = pl.ds(8 * m, 8)
        pltpu.make_async_copy(act.at[some], act_ref.at[some], act_sem.at[m]).start()
        return 0

    lax.fori_loop(0, 8, point, 0)
    outs = []
    for n in range(8):
        some = pl.ds(8 * n, 8)
        outs.append(pltpu.make_async_copy(act.at[some], act_ref.at[some], act_sem.at[n]))
    for n, (g, s) in enumerate(((g0, s0), (g1, s1))):

        def rows_of(t, _, g=g, s=s):
            for y in range(8):
                v = [s[pl.ds((t * 8 + m) * 64 + y * 8, 8), :] for m in range(8)]
                at = pl.multiple_of((t * 8 + y + 1) * CO, CO)
                g[pl.ds(at, CO), :] = jnp.concatenate(v, axis=0).astype(BF)
            return 0

        lax.fori_loop(0, NY // 8, rows_of, 0)
        first, second = (outer_ref, inner_ref) if n == 0 else (inner_ref, outer_ref)
        outs += by_core([((g, first), (g, second))], act_sem.at[pl.ds(8 + n, 1)])
    for out in outs:
        out.wait()


def weight_kernel(*refs):
    p_refs, g_refs, out_ref = refs[:4], refs[4:6], refs[6]
    planes, gs_buf, acc, sems = refs[7:11], refs[11:13], refs[13], refs[14]
    first, second = halves(x_sources(*p_refs), planes, CI, sems)
    g_first, g_second = halves(g_sources(*g_refs), gs_buf, CO, sems.at[pl.ds(8, 4)])
    acc[...] = jnp.zeros_like(acc)
    lane = lax.broadcasted_iota(jnp.int32, (CO, NX), 1)

    def rows(q, _):
        gs, xs = [], []
        for y in range(8):
            ystart = pl.multiple_of((8 * q + y) * CI, CI)
            gstart = pl.multiple_of((8 * q + y + 1) * CO, CO)
            for z, g in enumerate(gs_buf):
                mid = g[pl.ds(gstart, CO), :]
                wide = mid.astype(F32)
                before = jnp.where(lane == NX - 1, 0.0, pltpu.roll(wide, NX - 1, 1)).astype(BF)
                after = jnp.where(lane == 0, 0.0, pltpu.roll(wide, 1, 1)).astype(BF)
                gs.append(jnp.concatenate([before, mid, after], axis=0))
                xs.append(
                    jnp.concatenate(
                        [planes[z + i][pl.ds(ystart, 3 * CI), :] for i in range(3)]
                        + [jnp.ones((16, NX), BF)],
                        axis=0,
                    )
                )
        acc[...] += lax.dot_general(
            jnp.concatenate(xs, axis=1),
            jnp.concatenate(gs, axis=1),
            (((1,), (1,)), ((), ())),
            preferred_element_type=F32,
        )
        return 0

    for part, lo in ((first + g_first, 0), (second + g_second, 24)):
        for copy in part:
            copy.wait()
        lax.fori_loop(lo // 8, lo // 8 + 3, rows, 0)
    out_ref[0:288, :] = acc[0:288, 0:128].astype(BF)
    side = acc[0:288, 128:192]
    tail = jnp.concatenate([side[160:288], jnp.zeros((32, CO), F32)], axis=0)
    out_ref[288:448, :] = jnp.concatenate([side[0:160], tail], axis=1).astype(BF)
    out_ref[448:464, :] = acc[288:304, 0:128].astype(BF)
    out_ref[464:512, :] = jnp.zeros((48, NX), BF)


def add_rows(s, q, z_rows, fresh):
    for h in range(2):
        rr = z_rows[:, NX * h : NX * (h + 1)]
        y = shifted_sum(rr[128:192], rr[64:128], rr[0:64])
        for p in range(2):
            for m in range(4):
                at = pl.ds(row_of(4 * q + 2 * h + p, m, 4), 8)
                part = y[32 * p + 8 * m : 32 * p + 8 * m + 8]
                s[at, :] = part if fresh else s[at, :] + part


def window(g, q):
    sides = [g[pl.ds(pl.multiple_of((2 * q + h) * (2 * CO), 2 * CO), 4 * CO), :] for h in range(2)]
    return jnp.concatenate(sides, axis=1)


def back_kernel(inner_ref, outer_ref, d_ref, own0_ref, own1_ref, g0, g1, d, s0, s1, sems, out_sem):
    d_copy = pltpu.make_async_copy(d_ref, d, sems.at[4])
    d_copy.start()
    first, second = halves(g_sources(inner_ref, outer_ref), (g0, g1), CO, sems)

    def conv(q, _):
        r = jnp.dot(d[192:576, :], window(g0, q), preferred_element_type=F32)
        r += jnp.dot(d[0:384, :], window(g1, q), preferred_element_type=F32)
        add_rows(s0, q, r[0:192], True)
        add_rows(s1, q, r[192:384], True)
        return 0

    d_copy.wait()
    for part, lo in ((first, 0), (second, 6)):
        for copy in part:
            copy.wait()
        lax.fori_loop(lo, lo + 6, conv, 0, unroll=2)
    outs = []
    for n, (s, own) in enumerate(((s0, own0_ref), (s1, own1_ref))):
        outs.append(pltpu.make_async_copy(s, own, out_sem.at[n]))
        outs[-1].start()
    for out in outs:
        out.wait()


def finish_kernel(own0_ref, own1_ref, inner_ref, outer_ref, d_ref, out_ref, *rest):
    s0, s1, low, high, d, buf, sems, out_sem = rest
    first, second = halves(g_sources(inner_ref, outer_ref), (low, high), CO, sems)
    first.append(pltpu.make_async_copy(d_ref, d, sems.at[4]))
    first[-1].start()
    for n, (own, s) in enumerate(((own0_ref, s0), (own1_ref, s1))):
        first.append(pltpu.make_async_copy(own, s, sems.at[5 + n]))
        first[-1].start()

    def conv(q, _):
        r0 = jnp.dot(d[384:576, :], window(low, q), preferred_element_type=F32)
        r1 = jnp.dot(d[0:192, :], window(high, q), preferred_element_type=F32)
        add_rows(s0, q, r0, False)
        add_rows(s1, q, r1, False)
        return 0

    for part, lo in ((first, 0), (second, 6)):
        for copy in part:
            copy.wait()
        lax.fori_loop(lo, lo + 6, conv, 0, unroll=2)

    def gather(m, _):
        for n in range(8):
            for z, s in ((0, s0), (1, s1)):
                v = [s[pl.ds((t * 4 + m) * 64 + n, 8, stride=8), :] for t in range(NY // 8)]
                buf[m * 8 + n, z] = jnp.concatenate(v, axis=0).astype(BF)
        some = pl.ds(8 * m, 8)
        pltpu.make_async_copy(buf.at[some], out_ref.at[some], out_sem.at[m]).start()
        return 0

    lax.fori_loop(0, 4, gather, 0)
    for n in range(4):
        some = pl.ds(8 * n, 8)
        pltpu.make_async_copy(buf.at[some], out_ref.at[some], out_sem.at[n]).wait()


def prep_kernel(w_hbm, f_hbm, a_out, d_out, out_ref, turned, a_ref, d_ref, w_ref, f_ref, sem):
    w_copy = pltpu.make_async_copy(w_hbm, w_ref, sem.at[2])
    w_copy.start()
    f_copies = [
        pltpu.make_async_copy(f_hbm.at[pl.ds(512 * n, 512)], f_ref.at[pl.ds(512 * n, 512)], sem.at[3 + n])
        for n in range(4)
    ]
    for copy in f_copies:
        copy.start()
    w_copy.wait()
    for z, hole in ((0, 3), (1, 0)):
        for k in range(3):
            col = (k * 2 + z) * 128
            turned[hole * 128 : hole * 128 + 128, col : col + 128] = jnp.zeros((128, 128), F32)
    for i in range(3):
        for k in range(3):
            w = [w_ref[i, j, k].astype(F32) for j in range(3)]
            none = jnp.zeros((CI, CO), F32)
            for s in range(4):
                pair = jnp.concatenate([w[s] if s < 3 else none, w[s - 1] if s else none], axis=1)
                y, p = ((0, 1), (1, 1), (0, 0), (1, 0))[s]
                row, col = i * 192 + (k * 2 + y) * CI, p * 128
                d_ref[row : row + CI, col : col + 128] = pair.astype(BF)
                for z in range(2):
                    row, col = ((i + z) * 4 + s) * CI, (k * 2 + z) * 128
                    turned[row : row + CI, col : col + 128] = pair
    d_copy = pltpu.make_async_copy(d_ref, d_out, sem.at[0])
    d_copy.start()
    a_ref[...] = turned[...].T.astype(BF)
    a_copy = pltpu.make_async_copy(a_ref, a_out, sem.at[1])
    a_copy.start()
    for n, copy in enumerate(f_copies):
        copy.wait()
        part = f_ref[512 * n : 512 * n + 512, :]
        some = CHUNKS // 4
        out_ref[some * n : some * n + some] = part.reshape(some, FROWS, NX).astype(BF)
    d_copy.wait()
    a_copy.wait()


def join_b_kernel(f_ref, t_ref, out_ref):
    f = jnp.sum(f_ref[...].astype(F32), axis=0).astype(BF)
    t = jnp.sum(t_ref[...].astype(F32), axis=0).astype(BF)
    for n in range(COLS):
        out_ref[n, 0:FROWS] = f
        out_ref[n, FROWS:] = t


def join_c_kernel(in_ref, out_ref):
    both = jnp.sum(in_ref[...].astype(F32), axis=0).astype(BF)
    for n in range(CHUNKS):
        out_ref[n] = both


def out_kernel(in_ref, sum_ref, taps_ref, bias_ref):
    sum_ref[...] = in_ref[:, 0:FROWS, :].astype(F32).reshape(CHUNKS * FROWS, NX)
    scale = 1.0 / math.sqrt(8 * 64 * NY * NX)
    t = in_ref[:, FROWS:, :].astype(F32).reshape(CHUNKS * TROWS, NX) * scale
    for ij in range(9):
        two = t[ij * CI : ij * CI + CI]
        taps_ref[ij, 0] = two[:, 0:CO]
        taps_ref[ij, 1] = two[:, CO : 2 * CO]
        at, lane = (288 + ij * CI, 0) if ij < 5 else (288 + (ij - 5) * CI, CO)
        taps_ref[ij, 2] = t[at : at + CI, lane : lane + CO]
    bias_ref[...] = t[448:449, CO : 2 * CO]


def exchange(parts, axes):
    return lax.all_to_all(parts, axes, 0, 0)


def join_b(fin, taps):
    sds = jax.ShapeDtypeStruct((COLS, FROWS + TROWS, NX), BF)
    return call(join_b_kernel, sds, [], [VM] * 2, 1 << 20, 1 << 20)(fin, taps)


def join_c(parts):
    sds = jax.ShapeDtypeStruct((CHUNKS, FROWS + TROWS, NX), BF)
    return call(join_c_kernel, sds, [], [VM], 1 << 20, 1 << 20)(parts)


def swap(inner, outer):
    on_chip = [(i, i ^ 1) for i in range(32)]
    off_chip = [(i, i + 1) for i in range(1, 31, 2)] + [(i + 1, i) for i in range(1, 31, 2)]
    return lax.ppermute(inner, SPACE, on_chip), lax.ppermute(outer, SPACE, off_chip)


def far(x):
    return pltpu.with_memory_space_constraint(x, pltpu.HBM)


def layer(volumes, kernel, bias, cotangent, finished_grads):
    sds = jax.ShapeDtypeStruct
    x_plane = sds((PADY * CI, NX), BF)
    g_plane = sds((PADY * CO, NX), BF)
    turn = call(
        turn_kernel,
        (pltpu.HBM(x_plane.shape, BF), pltpu.HBM(x_plane.shape, BF)),
        [pltpu.VMEM((CI, 2, NY, NX), BF)]
        + [pltpu.VMEM((NY * CI, NX), F32)] * 2
        + [pltpu.VMEM((PADY * CI, NX), BF)] * 2
        + [DMA((4,)), DMA((2,))],
        [HBM],
        1 << 22,
        3 << 20,
        (HBM, HBM),
    )
    xbuf = pltpu.VMEM((PADY * CI, NX), BF)
    gbuf = pltpu.VMEM((PADY * CO, NX), BF)
    g_out = pltpu.HBM(g_plane.shape, BF)
    forward = call(
        forward_kernel,
        (pltpu.HBM((CO, 2, NY, NX), BF), g_out, g_out),
        [xbuf] * 4
        + [pltpu.VMEM((768, 512), BF)]
        + [pltpu.VMEM((CO, 2, NY, NX), BF)] * 2
        + [gbuf] * 2
        + [pltpu.VMEM((NY * CO, NX), F32)] * 2
        + [DMA((10,)), DMA((10,))],
        [ANY, ANY, HBM, HBM, HBM, pl.BlockSpec(memory_space=pltpu.SMEM), HBM],
        3 << 32,
        8 << 20,
        (HBM, HBM, HBM),
    )
    weight = call(
        weight_kernel,
        sds((512, NX), BF),
        [xbuf] * 4 + [gbuf] * 2 + [pltpu.VMEM((304, 192), F32), DMA((12,))],
        [ANY, ANY, HBM, HBM, HBM, HBM],
        3 << 32,
        5 << 20,
    )
    edge = (NY * CI, NX)
    dbuf = pltpu.VMEM((576, 256), BF)
    back = call(
        back_kernel,
        (pltpu.HBM(edge, F32), pltpu.HBM(edge, F32)),
        [gbuf] * 2 + [dbuf] + [pltpu.VMEM(edge, F32)] * 2 + [DMA((5,)), DMA((2,))],
        [HBM] * 3,
        2 << 32,
        6 << 20,
        (HBM,) * 2,
    )
    finish = call(
        finish_kernel,
        pltpu.HBM((CI, 2, NY, NX), BF),
        [pltpu.VMEM(edge, F32)] * 2
        + [gbuf] * 2
        + [dbuf, pltpu.VMEM((CI, 2, NY, NX), BF), DMA((7,)), DMA((4,))],
        [HBM, HBM, ANY, ANY, HBM],
        1 << 32,
        6 << 20,
        HBM,
    )
    prep = call(
        prep_kernel,
        (pltpu.HBM((768, 512), BF), pltpu.HBM((576, 256), BF), sds((CHUNKS, FROWS, NX), BF)),
        [
            pltpu.VMEM((512, 768), F32),
            pltpu.VMEM((768, 512), BF),
            pltpu.VMEM((576, 256), BF),
            pltpu.VMEM((3, 3, 3, CI, CO), BF),
            pltpu.VMEM((2048, NX), F32),
            DMA((7,)),
        ],
        [HBM] * 2,
        1 << 22,
        3 << 20,
        (HBM, HBM, VM),
    )
    out = call(
        out_kernel,
        (sds((CHUNKS * FROWS, NX), F32), sds((9, 3, CI, CO), F32), sds((1, CO), F32)),
        [],
        [VM],
        1 << 22,
        3 << 20,
    )
    inner, outer = turn(far(volumes[0]))
    far_inner, far_outer = swap(inner, outer)
    wf, wb, fin = prep(far(kernel.transpose(0, 1, 2, 4, 3)), far(finished_grads.reshape(2048, NX)))
    fin = exchange(fin, PLANE)
    x = (far_inner, far_outer, far(inner), far(outer))
    act, inner, outer = forward(*x, far(wf), bias, far(cotangent[0]))
    far_inner, far_outer = swap(inner, outer)
    taps = weight(*x, far(inner), far(outer))
    taps = exchange(taps.reshape(CHUNKS, TROWS, NX), PLANE)
    own0, own1 = back(far(inner), far(outer), far(wb))
    joined = join_b(fin, taps)
    joined = exchange(joined, COLUMN)
    joined = join_c(joined)
    joined = exchange(joined, PLANE)
    grad_volumes = finish(far(own0), far(own1), far_inner, far_outer, far(wb))
    summed, grad_taps, grad_bias = out(joined)
    grad_kernel = grad_taps.reshape(3, 3, 3, CI, CO).transpose(0, 1, 2, 4, 3)
    return act[None], grad_volumes[None], grad_kernel, grad_bias.reshape(CO), summed.reshape(-1)


def solution(mesh):
    fine = Mesh(mesh.devices.reshape(2, 4, 4, 2, 2, 2), ("yl", "x") + SPACE)
    dp = ("yl", "x")
    slab = P(dp, None, SPACE, None, None)
    return jax.shard_map(
        layer,
        mesh=fine,
        in_specs=(slab, P(), P(), slab, P(dp, SPACE, None)),
        out_specs=(slab, slab, P(), P(), P()),
        check_vma=False,
    )
```
